32 devices in a mesh: leaf: 4 (over z), dom: 2 (over core), rep: 4 (over y, x).
Axes of the slice: x: 2, y: 2, z: 4, core: 2. Of those that a mesh axis runs over, the one named last changes fastest.
Arguments:
- leaf_basis: bfloat16 [128, 512, 128], P(('leaf', 'dom', 'rep')), as said below
- transfer: float32 [224, 128, 128], P(('leaf', 'dom', 'rep')), as said below
- transfer_top: float32 [16, 128, 128], P(('leaf', 'dom')), as said below
- coupling_parts: bfloat16 [4, 512, 128, 128], P('rep', ('leaf', 'dom')), may hold values from -1 to 1
- row_slot: int32 [512], P(('leaf', 'dom', 'rep')), may hold values from 0 to 6, as said below
- col_node: int32 [512], P(('leaf', 'dom', 'rep')), may hold values from 0 to 223, as said below
Outputs:
- leaf_orth: bfloat16 [128, 512, 128], P(('leaf', 'dom', 'rep'))
- new_transfer: float32 [224, 128, 128], P(('leaf', 'dom', 'rep'))
- new_top: float32 [16, 128, 128], P(('leaf', 'dom'), 'rep')
- top_factor: float32 [8, 128, 128], P(('leaf', 'dom'), 'rep')
- coupling_new: bfloat16 [512, 128, 128], P(('leaf', 'dom', 'rep'))
The draws below stay inside these ranges and needn't reach their ends.
Inputs may be any that keep to these rules, and one draw needn't show every extreme that they name: `leaf_basis`: every leaf block has full column rank. Every transfer factor is invertible. `transfer_top`: every transfer factor is invertible. `row_slot`: slots 0 to 3 are the holding device's four leaves, 4 and 5 its two level-1 nodes, 6 its level-2 node; the holder of block k is device position k // 16 along leaf+dom+rep. col_node[k] = 7 d + c, where d is a device position along leaf+dom+rep at most 2 away from the holder of block k and c is a slot of the same level as row_slot[k] (0 to 3, 4 to 5, or 6); the first block of every device has its column node exactly 2 positions away.
All inputs are finite; a program needn't handle non-finite values.
Results may differ from the reference program's by a relative error of at most 0.013.
Values may be sent and summed in bfloat16 or wider, within the bound.
No kernel may reach another device: no remote copies, remote signals or barrier semaphores. Data moves between devices by JAX's collectives and lax.ppermute only.
A program may use at most 64 MiB of HBM per device.

```python
import math
import jax
import jax.numpy as jnp
from jax import lax

RANK = 128
PTS = 512
TILE_DEV = 16
REACH = 2
NLEAF = 128
TILES = 512
N_REP = 4


def draw_leaf_basis(key, part):
    base = jax.random.fold_in(key, 3)
    first_key, second_key, third_key, fourth_key, fifth_key = jax.random.split(base, 5)
    entries = jax.random.normal(first_key, (NLEAF, PTS, RANK), jnp.float32)
    scales = jnp.exp(jax.random.uniform(second_key, (NLEAF, RANK), jnp.float32, 0.0, math.log(3.0)))
    shared = jax.random.normal(fourth_key, (NLEAF, PTS), jnp.float32)
    loading = jax.random.uniform(fifth_key, (NLEAF, RANK), jnp.float32, 0.5, 1.5) * 0.5 * scales
    mixing = jax.random.normal(third_key, (NLEAF, RANK, RANK), jnp.float32) * (0.4 / math.sqrt(RANK))
    mixing = mixing + scales[:, :, None] * jnp.eye(RANK, dtype=jnp.float32)[None]
    independent = jnp.einsum('npr,nrs->nps', entries, mixing)
    return (independent + shared[:, :, None] * loading[:, None, :]).astype(jnp.bfloat16)


def transfer_like(key, count):
    noise = jax.random.normal(key, (count, RANK, RANK), jnp.float32)
    return noise * (0.25 / math.sqrt(RANK)) + 0.7 * jnp.eye(RANK, dtype=jnp.float32)[None]


def draw_transfer(key, part):
    return transfer_like(jax.random.fold_in(key, 5), 7 * (NLEAF // 4))


def draw_transfer_top(key, part):
    return transfer_like(jax.random.fold_in(key, 7), NLEAF // 8)


def tile_lists(key):
    base = jax.random.fold_in(key, 17)
    first_key, second_key, third_key, fourth_key = jax.random.split(base, 4)
    devices = TILES // TILE_DEV
    positions = jnp.arange(TILES, dtype=jnp.int32)
    holders = positions // TILE_DEV
    first_end = positions == TILE_DEV - 1
    last_end = positions == TILES - 1
    rows_drawn = jax.random.randint(first_key, (TILES,), 0, 7, dtype=jnp.int32)
    rows_drawn = jnp.where(first_end, 0, jnp.where(last_end, 6, rows_drawn))
    slot_pick = jax.random.randint(second_key, (TILES,), 0, 4, dtype=jnp.int32)
    slot_pick = jnp.where(first_end, 0, slot_pick)
    col_slots = jnp.where(rows_drawn < 4, slot_pick, jnp.where(rows_drawn < 6, 4 + slot_pick % 2, 6))
    offsets = jax.random.randint(third_key, (TILES,), -REACH, REACH + 1, dtype=jnp.int32)
    signs = jax.random.randint(fourth_key, (TILES,), 0, 2, dtype=jnp.int32) * 2 - 1
    offsets = jnp.where(positions % TILE_DEV == 0, signs * REACH, offsets)
    offsets = jnp.where(first_end | last_end, 0, offsets)
    target = holders + offsets
    target = jnp.where((target < 0) | (target >= devices), holders - offsets, target)
    return (rows_drawn, (7 * target + col_slots).astype(jnp.int32))


def draw_row_slot(key, part):
    return tile_lists(key)[0]


def draw_col_node(key, part):
    return tile_lists(key)[1]


def block_scale(rng, dims, cuts, smallest, top_value):
    def one(axis_at, shards_of):
        heights = jax.random.uniform(jax.random.fold_in(jax.random.fold_in(rng, 6), axis_at), (shards_of,), jnp.float32, smallest / len(cuts), top_value / len(cuts))
        return jnp.repeat(jnp.exp(heights), dims[axis_at] // shards_of).reshape((-1,) + (1,) * (len(dims) - axis_at - 1))

    factor_of = one(*cuts[0])
    for cut in cuts[1:]:
        factor_of = factor_of * one(*cut)
    return factor_of


def bell_draw(key, shape, spread, most, cuts=(), kind=jnp.bfloat16):
    drawn = spread * jax.random.normal(key, shape, jnp.float32)
    if cuts:
        drawn = drawn * block_scale(key, shape, cuts, -0.22, 0.18)
    return jnp.clip(drawn, -most, most).astype(kind)


def setup_inputs(seed: int = 0) -> dict:
    splits = jax.random.split(jax.random.key(seed), 7)
    leaf_basis = draw_leaf_basis(jax.random.fold_in(splits[6], 71), 0)
    transfer = draw_transfer(jax.random.fold_in(splits[6], 71), 0)
    transfer_top = draw_transfer_top(jax.random.fold_in(splits[6], 71), 0)
    coupling_parts = bell_draw(splits[3], (N_REP, TILES, RANK, RANK), 0.15, 1.0, ((0, 4), (1, 8)))
    row_slot = draw_row_slot(jax.random.fold_in(splits[6], 71), 0)
    col_node = draw_col_node(jax.random.fold_in(splits[6], 71), 0)
    return {"leaf_basis": leaf_basis, "transfer": transfer, "transfer_top": transfer_top, "coupling_parts": coupling_parts, "row_slot": row_slot, "col_node": col_node}


def precise(first, second):
    return jnp.dot(first.astype(jnp.float32), second.astype(jnp.float32), precision=lax.Precision.HIGHEST, preferred_element_type=jnp.float32)

def lower_solve(low_factor, rhs_mat):
    return lax.linalg.triangular_solve(low_factor, rhs_mat, left_side=True, lower=True)

def leaf_factor(leaf_rows):
    gram_sum = jnp.dot(leaf_rows.T.astype(jnp.float32), leaf_rows.astype(jnp.float32), preferred_element_type=jnp.float32) * (1.0 / PTS)
    low_factor = jnp.linalg.cholesky(gram_sum)
    identity = jnp.eye(gram_sum.shape[0], dtype=jnp.float32)
    inverse = lower_solve(low_factor, identity).T.astype(jnp.bfloat16)
    orthogonal = jnp.dot(leaf_rows.astype(jnp.float32), inverse.astype(jnp.float32), preferred_element_type=jnp.float32).astype(jnp.bfloat16)
    return (orthogonal, low_factor.T)

def combine(factor_a, factor_b, trans_a, trans_b):
    weighted_a = precise(factor_a, trans_a)
    weighted_b = precise(factor_b, trans_b)
    gram_sum = precise(weighted_a.T, weighted_a) + precise(weighted_b.T, weighted_b)
    low_factor = jnp.linalg.cholesky(gram_sum)
    new_first = lower_solve(low_factor, weighted_a.T).T
    new_second = lower_solve(low_factor, weighted_b.T).T
    return (low_factor.T, new_first, new_second)

def reference(leaf_basis, transfer, transfer_top, coupling_parts, row_slot, col_node):
    devices = transfer.shape[0] // 7
    rank_dim = transfer.shape[1]
    orthogonal, leaf_r = jax.vmap(leaf_factor)(leaf_basis)
    grouped = transfer.reshape(devices, 7, rank_dim, rank_dim)
    level_trans = [grouped[:, :4].reshape(4 * devices, rank_dim, rank_dim), grouped[:, 4:6].reshape(2 * devices, rank_dim, rank_dim), grouped[:, 6], transfer_top]
    factors = [leaf_r]
    renewed = []
    current = leaf_r
    for level_no in range(4):
        children = level_trans[level_no]
        parent, new_first, new_second = jax.vmap(combine)(current[0::2], current[1::2], children[0::2], children[1::2])
        renewed.append(jnp.stack([new_first, new_second], axis=1).reshape(children.shape))
        factors.append(parent)
        current = parent
    new_transfer = jnp.concatenate([renewed[0].reshape(devices, 4, rank_dim, rank_dim), renewed[1].reshape(devices, 2, rank_dim, rank_dim), renewed[2].reshape(devices, 1, rank_dim, rank_dim)], axis=1).reshape(7 * devices, rank_dim, rank_dim)
    factor_pool = jnp.concatenate([factors[0].reshape(devices, 4, rank_dim, rank_dim), factors[1].reshape(devices, 2, rank_dim, rank_dim), factors[2].reshape(devices, 1, rank_dim, rank_dim)], axis=1).reshape(7 * devices, rank_dim, rank_dim).astype(jnp.bfloat16)
    part_blocks = jnp.moveaxis(coupling_parts.reshape(N_REP, devices, TILE_DEV, rank_dim, rank_dim), 0, 1)
    row_blocks = row_slot.reshape(devices, TILE_DEV)
    col_blocks = col_node.reshape(devices, TILE_DEV)

    def project(block):
        holder, partials, rows_here, cols_here = block
        summed = jnp.sum(partials.astype(jnp.float32), axis=0).astype(jnp.bfloat16)
        left_factor = jnp.take(factor_pool, holder * 7 + rows_here, axis=0)
        right_factor = jnp.take(factor_pool, cols_here, axis=0)
        half_tile = jnp.einsum('kab,kbc->kac', left_factor.astype(jnp.float32), summed.astype(jnp.float32)).astype(jnp.bfloat16)
        return jnp.einsum('kab,kcb->kac', half_tile.astype(jnp.float32), right_factor.astype(jnp.float32)).astype(jnp.bfloat16)
    holders = jnp.arange(devices, dtype=jnp.int32)
    projected = lax.map(project, (holders, part_blocks, row_blocks, col_blocks))
    projected = projected.reshape(devices * TILE_DEV, rank_dim, rank_dim)
    return (orthogonal, new_transfer, renewed[3], factors[4], projected)
```

```python
import functools

import jax
import jax.numpy as jnp
from jax import lax
from jax.experimental import pallas as pl
from jax.experimental.pallas import tpu as pltpu
from jax.sharding import PartitionSpec as P

PTS = 512
REACH = 2
PANEL = 8
ALL = ("leaf", "dom", "rep")
F32 = jnp.float32
BF16 = jnp.bfloat16
VMEM = pl.BlockSpec(memory_space=pltpu.VMEM)
SMEM = pl.BlockSpec(memory_space=pltpu.SMEM)
ANY = pl.BlockSpec(memory_space=pl.ANY)


def dot_nn(a, b):
    return lax.dot_general(
        a, b, (((1,), (0,)), ((), ())),
        precision=lax.Precision.HIGHEST, preferred_element_type=F32,
    )


def dot_tn(a, b):
    return lax.dot_general(
        a, b, (((0,), (0,)), ((), ())),
        precision=lax.Precision.HIGHEST, preferred_element_type=F32,
    )


def dot_nt(a, b):
    return lax.dot_general(
        a, b, (((1,), (1,)), ((), ())),
        precision=lax.Precision.HIGHEST, preferred_element_type=F32,
    )


def congruence(gram, trans):
    return dot_tn(trans, dot_nn(gram, trans))


def split3(x):
    high = x.astype(BF16).astype(F32)
    rest = x - high
    mid = rest.astype(BF16).astype(F32)
    return high, mid, rest - mid


def factorize(work, upper, inverse, mats):
    size = work.shape[-1]
    shape = (PANEL, size)
    sub = lax.broadcasted_iota(jnp.int32, shape, 0)
    lane = lax.broadcasted_iota(jnp.int32, shape, 1)

    def row(value, at):
        return jnp.broadcast_to(value[at : at + 1, :], shape)

    for start in range(0, size, PANEL):
        stop = start + PANEL
        in_panel = (lane >= start) & (lane < stop)
        eye = (lane == sub + start).astype(F32)
        tops = [work[m, start:stop, :] for m in mats]
        cols = [
            [jnp.broadcast_to(top[:, start + k : start + k + 1], shape) for k in range(PANEL)]
            for top in tops
        ]
        both = [jnp.where(in_panel, eye, top) for top in tops]
        for j in range(PANEL):
            for t in range(len(mats)):
                scale = lax.rsqrt(row(cols[t][j], j))
                low = cols[t][j] * scale
                below = jnp.where(sub > j, low, 0.0)
                for k in range(j + 1, PANEL):
                    cols[t][k] = cols[t][k] - below * row(low, k)
                pivot = row(tops[t], j) * scale
                tops[t] = jnp.where(sub == j, pivot, tops[t] - below * pivot)
                pivot = row(both[t], j) * scale
                both[t] = jnp.where(sub == j, pivot, both[t] - below * pivot)
        for t, m in enumerate(mats):
            upper[m, start:stop, :] = jnp.where(lane >= sub + start, tops[t], 0.0)
            inverse[m, start:stop, :] = jnp.where(lane < stop, both[t], 0.0)
            if stop < size:
                high, mid, low = split3(both[t])
                left = jnp.concatenate([high, high, mid, mid, high, low], axis=0)
                right = jnp.concatenate([high, mid, high, mid, low, high], axis=0)
                update = lax.dot_general(
                    left.astype(BF16), right.astype(BF16), (((0,), (0,)), ((), ())),
                    preferred_element_type=F32,
                )
                rest = lax.broadcasted_iota(jnp.int32, (size - stop, size), 1)
                drop = (rest >= start) & (rest < stop)
                old = jnp.where(drop, 0.0, work[m, stop:, :])
                work[m, stop:, :] = old - update[stop:, :]


def gram_kernel(basis, trans, grams, sent):
    leaves = basis.shape[0]
    for i in range(leaves):
        rows = basis[i]
        grams[i] = lax.dot_general(
            rows, rows, (((0,), (0,)), ((), ())), preferred_element_type=F32
        ) * (1.0 / PTS)
    base, count = 0, leaves
    while count > 1:
        for pair in range(count // 2):
            one, two = base + 2 * pair, base + 2 * pair + 1
            grams[base + count + pair] = congruence(grams[one], trans[one]) + congruence(
                grams[two], trans[two]
            )
        base, count = base + count, count // 2
    sent[...] = congruence(grams[base], trans[base])


def factor_kernel(rep, grams, own, near, far_a, far_b, trans_top, pool, upper, inverse, work):
    slots = grams.shape[0]
    high = rep[0] // 2
    mine = own[...] + near[...]
    other = far_a[...] + far_b[...]
    three_a = jnp.where(high == 0, mine, other)
    three_b = jnp.where(high == 0, other, mine)
    work[:slots] = grams[...]
    work[slots] = three_a
    work[slots + 1] = three_b
    work[slots + 2] = congruence(three_a, trans_top[0]) + congruence(three_b, trans_top[1])
    factorize(work, upper, inverse, list(range(slots + 3)))
    pool[...] = upper[:slots].astype(BF16)


def finish_kernel(rep, basis, trans, trans_top, upper, inverse, orth, fresh, top, four):
    leaves = basis.shape[0]
    for i in range(leaves):
        orth[i] = lax.dot_general(
            basis[i], inverse[i].astype(BF16), (((1,), (1,)), ((), ())),
            preferred_element_type=F32,
        ).astype(BF16)
    base, count = 0, leaves
    while count > 1:
        for child in range(count):
            node = base + child
            fresh[node] = dot_nt(
                dot_nn(upper[node], trans[node]), inverse[base + count + child // 2]
            )
        base, count = base + count, count // 2
    share = four.shape[1]
    rows = pl.ds(pl.multiple_of(rep[0] * share, share), share)
    three = base + 1
    own_three = inverse[three + rep[0] // 2]
    fresh[base] = dot_nt(dot_nn(upper[base], trans[base]), own_three)
    for c in range(2):
        top[c] = dot_nt(dot_nn(upper[three + c, rows, :], trans_top[c]), inverse[three + 2])
    four[0] = upper[three + 2, rows, :]


def project_kernel(row_slot, col_at, got, *refs):
    pieces, (out, pool, sem) = refs[: 2 * REACH + 1], refs[2 * REACH + 1 :]
    slots = pieces[0].shape[0]
    tiles = out.shape[0]
    copies = [
        pltpu.make_async_copy(piece, pool.at[pl.ds(i * slots, slots)], sem.at[i])
        for i, piece in enumerate(pieces)
    ]
    for copy in copies:
        copy.start()
    for copy in copies:
        copy.wait()
    for k in range(tiles):
        total = got[0, k].astype(F32)
        for i in range(1, got.shape[0]):
            total = total + got[i, k].astype(F32)
        half = jnp.dot(
            pool[REACH * slots + row_slot[k]], total.astype(BF16), preferred_element_type=F32
        ).astype(BF16)
        out[k] = lax.dot_general(
            half, pool[col_at[k]], (((1,), (1,)), ((), ())), preferred_element_type=F32
        ).astype(BF16)


def from_behind(value, axis, steps):
    count = lax.axis_size(axis)
    leading, last = (max(0, -steps), min(count, count - steps))
    return lax.ppermute(value, axis, [(source, source + steps) for source in range(leading, last)])


def swapped(value, flip):
    return lax.ppermute(value, "rep", [(i, i ^ flip) for i in range(lax.axis_size("rep"))])


def per_device(leaf_basis, transfer, transfer_top, coupling_parts, row_slot, col_node):
    rank = transfer.shape[1]
    slots = transfer.shape[0]
    leaves = leaf_basis.shape[0]
    reps = lax.axis_size("rep")
    tiles = row_slot.shape[0]
    square = (rank, rank)
    rep = lax.axis_index("rep").astype(jnp.int32).reshape(1)

    got = lax.all_to_all(
        coupling_parts.reshape(reps, tiles, rank, rank), "rep", 0, 0, tiled=True
    )

    grams, sent = pl.pallas_call(
        gram_kernel,
        out_shape=[
            jax.ShapeDtypeStruct((slots, *square), F32),
            jax.ShapeDtypeStruct(square, F32),
        ],
        in_specs=[VMEM, VMEM],
        out_specs=[VMEM, VMEM],
        name="grams",
    )(leaf_basis, transfer)
    near, far_a, far_b = (swapped(sent, flip) for flip in (1, 2, 3))
    pool, upper, inverse = pl.pallas_call(
        factor_kernel,
        out_shape=[
            jax.ShapeDtypeStruct((slots, *square), BF16),
            jax.ShapeDtypeStruct((slots + 3, *square), F32),
            jax.ShapeDtypeStruct((slots + 3, *square), F32),
        ],
        in_specs=[SMEM] + [VMEM] * 6,
        out_specs=[VMEM] * 3,
        scratch_shapes=[pltpu.VMEM((slots + 3, *square), F32)],
        name="factor",
    )(rep, grams, sent, near, far_a, far_b, transfer_top)
    pieces = [
        pool if offset == 0 else from_behind(pool, ALL, -offset)
        for offset in range(-REACH, REACH + 1)
    ]
    share = rank // reps
    orth, fresh, top, four = pl.pallas_call(
        finish_kernel,
        out_shape=[
            jax.ShapeDtypeStruct(leaf_basis.shape, BF16),
            jax.ShapeDtypeStruct(transfer.shape, F32),
            jax.ShapeDtypeStruct((2, share, rank), F32),
            jax.ShapeDtypeStruct((1, share, rank), F32),
        ],
        in_specs=[SMEM] + [VMEM] * 5,
        out_specs=[VMEM] * 4,
        name="finish",
    )(rep, leaf_basis, transfer, transfer_top, upper, inverse)
    my_index = lax.axis_index(ALL)
    col_at = (col_node // slots - my_index + REACH) * slots + col_node % slots
    projected = pl.pallas_call(
        project_kernel,
        out_shape=jax.ShapeDtypeStruct((tiles, *square), BF16),
        in_specs=[SMEM] * 2 + [VMEM] + [ANY] * (2 * REACH + 1),
        out_specs=VMEM,
        scratch_shapes=[
            pltpu.VMEM(((2 * REACH + 1) * slots, *square), BF16),
            pltpu.SemaphoreType.DMA((2 * REACH + 1,)),
        ],
        name="project",
    )(row_slot, col_at, got, *pieces)
    return (orth, fresh, top, four, projected)


def solution(mesh):
    return jax.shard_map(
        per_device,
        mesh=mesh,
        in_specs=(
            P(ALL, None, None),
            P(ALL, None, None),
            P(("leaf", "dom"), None, None),
            P("rep", ("leaf", "dom"), None, None),
            P(ALL),
            P(ALL),
        ),
        out_specs=(
            P(ALL, None, None),
            P(ALL, None, None),
            P(("leaf", "dom"), "rep", None),
            P(("leaf", "dom"), "rep", None),
            P(ALL, None, None),
        ),
        check_vma=False,
    )
```

```python
import functools

import jax
import jax.numpy as jnp
from jax import lax
from jax.experimental import pallas as pl
from jax.experimental.pallas import tpu as pltpu
from jax.sharding import PartitionSpec as P


PTS = 512
REACH = 2
PANEL = 8
TILE = 16
ALL = ("leaf", "dom", "rep")
F32 = jnp.float32
BF16 = jnp.bfloat16
VMEM = pl.BlockSpec(memory_space=pltpu.VMEM)
SMEM = pl.BlockSpec(memory_space=pltpu.SMEM)
ANY = pl.BlockSpec(memory_space=pl.ANY)
PARAMS = pltpu.CompilerParams(vmem_limit_bytes=16 * 1024 * 1024)


def dot_nn(a, b):
    return lax.dot_general(
        a, b, (((1,), (0,)), ((), ())),
        precision=lax.Precision.HIGHEST, preferred_element_type=F32,
    )


def dot_tn(a, b):
    return lax.dot_general(
        a, b, (((0,), (0,)), ((), ())),
        precision=lax.Precision.HIGHEST, preferred_element_type=F32,
    )


def dot_nt(a, b):
    return lax.dot_general(
        a, b, (((1,), (1,)), ((), ())),
        precision=lax.Precision.HIGHEST, preferred_element_type=F32,
    )


def congruence(gram, trans):
    return dot_tn(trans, dot_nn(gram, trans))


def split3(x):
    high = x.astype(BF16).astype(F32)
    rest = x - high
    mid = rest.astype(BF16).astype(F32)
    return high, mid, rest - mid


def factorize(work, upper, inverse, mats):
    size = work.shape[-1]
    shape = (PANEL, size)
    sub = lax.broadcasted_iota(jnp.int32, shape, 0)
    lane = lax.broadcasted_iota(jnp.int32, shape, 1)

    def row(value, at):
        return jnp.broadcast_to(value[at : at + 1, :], shape)

    for start in range(0, size, PANEL):
        stop = start + PANEL
        in_panel = (lane >= start) & (lane < stop)
        eye = (lane == sub + start).astype(F32)
        tops = [work[m, start:stop, :] for m in mats]
        cols = [
            [jnp.broadcast_to(top[:, start + k : start + k + 1], shape) for k in range(PANEL)]
            for top in tops
        ]
        both = [jnp.where(in_panel, eye, top) for top in tops]
        for j in range(PANEL):
            for t in range(len(mats)):
                scale = lax.rsqrt(row(cols[t][j], j))
                low = cols[t][j] * scale
                below = jnp.where(sub > j, low, 0.0)
                for k in range(j + 1, PANEL):
                    cols[t][k] = cols[t][k] - below * row(low, k)
                pivot = row(tops[t], j) * scale
                tops[t] = jnp.where(sub == j, pivot, tops[t] - below * pivot)
                pivot = row(both[t], j) * scale
                both[t] = jnp.where(sub == j, pivot, both[t] - below * pivot)
        for t, m in enumerate(mats):
            upper[m, start:stop, :] = jnp.where(lane >= sub + start, tops[t], 0.0)
            inverse[m, start:stop, :] = jnp.where(lane < stop, both[t], 0.0)
            if stop < size:
                high, mid, low = split3(both[t])
                left = jnp.concatenate([high, high, mid, mid, high, low], axis=0)
                right = jnp.concatenate([high, mid, high, mid, low, high], axis=0)
                update = lax.dot_general(
                    left.astype(BF16), right.astype(BF16), (((0,), (0,)), ((), ())),
                    preferred_element_type=F32,
                )
                rest = lax.broadcasted_iota(jnp.int32, (size - stop, size), 1)
                drop = (rest >= start) & (rest < stop)
                old = jnp.where(drop, 0.0, work[m, stop:, :])
                work[m, stop:, :] = old - update[stop:, :]


def gram_kernel(basis, trans, grams, sent):
    leaves = basis.shape[0]
    for i in range(leaves):
        rows = basis[i]
        grams[i] = lax.dot_general(
            rows, rows, (((0,), (0,)), ((), ())), preferred_element_type=F32
        ) * (1.0 / PTS)
    base, count = 0, leaves
    while count > 1:
        for pair in range(count // 2):
            one, two = base + 2 * pair, base + 2 * pair + 1
            grams[base + count + pair] = congruence(grams[one], trans[one]) + congruence(
                grams[two], trans[two]
            )
        base, count = base + count, count // 2
    sent[...] = congruence(grams[base], trans[base])


def factor_kernel(
    rep, grams, own, near, far_a, far_b, trans_top, packed, pool, upper, inverse, work
):
    slots = grams.shape[0]
    size = grams.shape[1]
    high = rep[0] // 2
    mine = own[...] + near[...]
    other = far_a[...] + far_b[...]
    three_a = jnp.where(high == 0, mine, other)
    three_b = jnp.where(high == 0, other, mine)
    work[:slots] = grams[...]
    work[slots] = three_a
    work[slots + 1] = three_b
    work[slots + 2] = congruence(three_a, trans_top[0]) + congruence(three_b, trans_top[1])
    factorize(work, upper, inverse, list(range(slots + 3)))
    pool[...] = upper[:slots].astype(BF16)
    sub = lax.broadcasted_iota(jnp.int32, (size, size), 0)
    lane = lax.broadcasted_iota(jnp.int32, (size, size), 1)
    pairs = (slots + 1) // 2
    for even in range(0, slots, 2):
        square = upper[even]
        if even + 1 < slots:
            odd = upper[even + 1]
            square = jnp.where(lane >= sub, square, odd.T)
            diagonal = jnp.sum(jnp.where(lane == sub, odd, 0.0), axis=0, keepdims=True)
            at = pairs * size + even // 2 * TILE
            packed[at : at + TILE, :] = jnp.broadcast_to(diagonal, (TILE, size)).astype(BF16)
        at = even // 2 * size
        packed[at : at + size, :] = square.astype(BF16)


def finish_kernel(rep, basis, trans, trans_top, upper, inverse, orth, fresh, top, four):
    leaves = basis.shape[0]
    for i in range(leaves):
        orth[i] = lax.dot_general(
            basis[i], inverse[i].astype(BF16), (((1,), (1,)), ((), ())),
            preferred_element_type=F32,
        ).astype(BF16)
    base, count = 0, leaves
    while count > 1:
        for child in range(count):
            node = base + child
            fresh[node] = dot_nt(
                dot_nn(upper[node], trans[node]), inverse[base + count + child // 2]
            )
        base, count = base + count, count // 2
    share = four.shape[1]
    rows = pl.ds(pl.multiple_of(rep[0] * share, share), share)
    three = base + 1
    own_three = inverse[three + rep[0] // 2]
    fresh[base] = dot_nt(dot_nn(upper[base], trans[base]), own_three)
    for c in range(2):
        top[c] = dot_nt(dot_nn(upper[three + c, rows, :], trans_top[c]), inverse[three + 2])
    four[0] = upper[three + 2, rows, :]


def cut_kernel(rep, parts, lead, tail, sem):
    me = rep[0]
    copies = [
        pltpu.make_async_copy(parts.at[me ^ flip, which], out.at[at], sem.at[2 * which + at])
        for which, (out, flips) in enumerate(((lead, (1, 3)), (tail, (2, 3))))
        for at, flip in enumerate(flips)
    ]
    for copy in copies:
        copy.start()
    for copy in copies:
        copy.wait()


def fold_kernel(rep, parts, lead, tail, lead_sum, tail_sum, own, sem):
    me = rep[0]
    copies = [
        pltpu.make_async_copy(parts.at[me ^ flip, which], own.at[which], sem.at[which])
        for which, flip in enumerate((2, 1))
    ]
    for copy in copies:
        copy.start()
    for which, (came, out) in enumerate(((lead, lead_sum), (tail, tail_sum))):
        copies[which].wait()
        out[...] = (came[1].astype(F32) + own[which].astype(F32)).astype(BF16)


def half_kernel(rep, row_slot, parts, lead, tail, lead_rest, tail_rest, pool, half, own, sem):
    copy = pltpu.make_async_copy(parts.at[rep[0]], own, sem)
    copy.start()
    copy.wait()
    for which, (near, rest) in enumerate(((lead, lead_rest), (tail, tail_rest))):
        for i in range(rest.shape[0]):
            total = own[which, i].astype(F32) + near[0, i].astype(F32) + rest[i].astype(F32)
            k = which * rest.shape[0] + i
            half[k] = jnp.dot(
                pool[row_slot[k]], total.astype(BF16), preferred_element_type=F32
            ).astype(BF16)


def project_kernel(slots, mine, col_node, half, *refs):
    count = 2 * REACH + 1
    pieces, (out, pool, sem) = refs[:count], refs[count:]
    rows = pieces[0].shape[0]
    size = out.shape[1]
    copies = [
        pltpu.make_async_copy(piece, pool.at[pl.ds(i * rows, rows)], sem.at[i])
        for i, piece in enumerate(pieces)
    ]
    for copy in copies:
        copy.start()
    sub = lax.broadcasted_iota(jnp.int32, (size, size), 0)
    lane = lax.broadcasted_iota(jnp.int32, (size, size), 1)
    above = (lane >= sub).astype(F32).astype(BF16)
    below = (lane < sub).astype(F32).astype(BF16)
    eye = (lane == sub).astype(F32).astype(BF16)
    pairs = (slots + 1) // 2
    for copy in copies:
        copy.wait()
    for k in range(out.shape[0]):
        piece, slot = col_node[k] // slots - mine[0] + REACH, col_node[k] % slots
        base = piece * rows
        square = pool[pl.ds(pl.multiple_of(base + slot // 2 * size, TILE), size), :]
        spot = jnp.minimum(slot // 2, slots // 2 - 1)
        at = pl.multiple_of(base + pairs * size + spot * TILE, TILE)
        diagonal = jnp.concatenate([pool[pl.ds(at, TILE), :]] * (size // TILE), axis=0)
        even = lax.dot_general(
            half[k], square * above, (((1,), (1,)), ((), ())), preferred_element_type=F32
        )
        odd = jnp.dot(half[k], square * below + diagonal * eye, preferred_element_type=F32)
        out[k] = jnp.where(slot % 2 == 0, even, odd).astype(BF16)


def shifted(value, steps):
    count = lax.axis_size(ALL)
    return lax.ppermute(value, ALL, [(i, (i + steps) % count) for i in range(count)])


def swapped(value, flip):
    return lax.ppermute(value, "rep", [(i, i ^ flip) for i in range(lax.axis_size("rep"))])


def per_device(leaf_basis, transfer, transfer_top, coupling_parts, row_slot, col_node):
    rank = transfer.shape[1]
    slots = transfer.shape[0]
    reps = lax.axis_size("rep")
    tiles = row_slot.shape[0]
    square = (rank, rank)
    rep = lax.axis_index("rep").astype(jnp.int32).reshape(1)

    grams, sent = pl.pallas_call(
        gram_kernel,
        out_shape=[
            jax.ShapeDtypeStruct((slots, *square), F32),
            jax.ShapeDtypeStruct(square, F32),
        ],
        in_specs=[VMEM, VMEM],
        out_specs=[VMEM, VMEM],
        compiler_params=PARAMS,
        name="grams",
    )(leaf_basis, transfer)
    near, far_a, far_b = (swapped(sent, flip) for flip in (1, 2, 3))
    parts = coupling_parts.reshape(reps, 2, tiles // 2, rank, rank)
    pair = jax.ShapeDtypeStruct((2, tiles // 2, *square), BF16)
    single = jax.ShapeDtypeStruct((tiles // 2, *square), BF16)
    lead_out, tail_out = pl.pallas_call(
        cut_kernel,
        out_shape=[pair, pair],
        in_specs=[SMEM, ANY],
        out_specs=[VMEM, VMEM],
        scratch_shapes=[pltpu.SemaphoreType.DMA((4,))],
        compiler_params=PARAMS,
        name="cut",
    )(rep, parts)
    lead = swapped(lead_out, 1)
    tail = swapped(tail_out, 2)
    lead_sum, tail_sum = pl.pallas_call(
        fold_kernel,
        out_shape=[single, single],
        in_specs=[SMEM, ANY, VMEM, VMEM],
        out_specs=[VMEM, VMEM],
        scratch_shapes=[pltpu.VMEM(pair.shape, BF16), pltpu.SemaphoreType.DMA((2,))],
        compiler_params=PARAMS,
        name="fold",
    )(rep, parts, lead, tail)
    lead_rest = swapped(lead_sum, 2)
    tail_rest = swapped(tail_sum, 1)
    pairs = (slots + 1) // 2
    packed, pool, upper, inverse = pl.pallas_call(
        factor_kernel,
        out_shape=[
            jax.ShapeDtypeStruct((pairs * rank + slots // 2 * TILE, rank), BF16),
            jax.ShapeDtypeStruct((slots, *square), BF16),
            jax.ShapeDtypeStruct((slots + 3, *square), F32),
            jax.ShapeDtypeStruct((slots + 3, *square), F32),
        ],
        in_specs=[SMEM] + [VMEM] * 6,
        out_specs=[VMEM] * 4,
        scratch_shapes=[pltpu.VMEM((slots + 3, *square), F32)],
        compiler_params=PARAMS,
        name="factor",
    )(rep, grams, sent, near, far_a, far_b, transfer_top)
    pieces = [
        packed if offset == 0 else shifted(packed, -offset)
        for offset in range(-REACH, REACH + 1)
    ]
    share = rank // reps
    orth, fresh, top, four = pl.pallas_call(
        finish_kernel,
        out_shape=[
            jax.ShapeDtypeStruct(leaf_basis.shape, BF16),
            jax.ShapeDtypeStruct(transfer.shape, F32),
            jax.ShapeDtypeStruct((2, share, rank), F32),
            jax.ShapeDtypeStruct((1, share, rank), F32),
        ],
        in_specs=[SMEM] + [VMEM] * 5,
        out_specs=[VMEM] * 4,
        compiler_params=PARAMS,
        name="finish",
    )(rep, leaf_basis, transfer, transfer_top, upper, inverse)
    half = pl.pallas_call(
        half_kernel,
        out_shape=jax.ShapeDtypeStruct((tiles, *square), BF16),
        in_specs=[SMEM, SMEM, ANY] + [VMEM] * 5,
        out_specs=VMEM,
        scratch_shapes=[
            pltpu.VMEM((2, tiles // 2, *square), BF16),
            pltpu.SemaphoreType.DMA,
        ],
        compiler_params=PARAMS,
        name="half",
    )(rep, row_slot, parts, lead, tail, lead_rest, tail_rest, pool)
    mine = lax.axis_index(ALL).astype(jnp.int32).reshape(1)
    projected = pl.pallas_call(
        functools.partial(project_kernel, slots),
        out_shape=jax.ShapeDtypeStruct((tiles, *square), BF16),
        in_specs=[SMEM, SMEM, VMEM] + [ANY] * (2 * REACH + 1),
        out_specs=VMEM,
        scratch_shapes=[
            pltpu.VMEM(((2 * REACH + 1) * packed.shape[0], rank), BF16),
            pltpu.SemaphoreType.DMA((2 * REACH + 1,)),
        ],
        compiler_params=PARAMS,
        name="project",
    )(mine, col_node, half, *pieces)
    return (orth, fresh, top, four, projected)


def solution(mesh):
    return jax.shard_map(
        per_device,
        mesh=mesh,
        in_specs=(
            P(ALL, None, None),
            P(ALL, None, None),
            P(("leaf", "dom"), None, None),
            P("rep", ("leaf", "dom"), None, None),
            P(ALL),
            P(ALL),
        ),
        out_specs=(
            P(ALL, None, None),
            P(ALL, None, None),
            P(("leaf", "dom"), "rep", None),
            P(("leaf", "dom"), "rep", None),
            P(ALL, None, None),
        ),
        check_vma=False,
    )
```

```python
import functools

import jax
import jax.numpy as jnp
from jax import lax
from jax.experimental import pallas as pl
from jax.experimental.pallas import tpu as pltpu
from jax.sharding import PartitionSpec as P


PTS = 512
REACH = 2
PANEL = 8
TILE = 16
ALL = ("leaf", "dom", "rep")
F32 = jnp.float32
BF16 = jnp.bfloat16
VMEM = pl.BlockSpec(memory_space=pltpu.VMEM)
SMEM = pl.BlockSpec(memory_space=pltpu.SMEM)
ANY = pl.BlockSpec(memory_space=pl.ANY)
PARAMS = pltpu.CompilerParams(vmem_limit_bytes=16 * 1024 * 1024)


def dot_nn(a, b):
    return lax.dot_general(
        a, b, (((1,), (0,)), ((), ())),
        precision=lax.Precision.HIGHEST, preferred_element_type=F32,
    )


def dot_tn(a, b):
    return lax.dot_general(
        a, b, (((0,), (0,)), ((), ())),
        precision=lax.Precision.HIGHEST, preferred_element_type=F32,
    )


def dot_nt(a, b):
    return lax.dot_general(
        a, b, (((1,), (1,)), ((), ())),
        precision=lax.Precision.HIGHEST, preferred_element_type=F32,
    )


def congruence(gram, trans):
    return dot_tn(trans, dot_nn(gram, trans))


def split3(x):
    high = x.astype(BF16).astype(F32)
    rest = x - high
    mid = rest.astype(BF16).astype(F32)
    return high, mid, rest - mid


def factorize(work, upper, inverse, mats):
    size = work.shape[-1]
    shape = (PANEL, size)
    sub = lax.broadcasted_iota(jnp.int32, shape, 0)
    lane = lax.broadcasted_iota(jnp.int32, shape, 1)

    def row(value, at):
        return jnp.broadcast_to(value[at : at + 1, :], shape)

    for start in range(0, size, PANEL):
        stop = start + PANEL
        in_panel = (lane >= start) & (lane < stop)
        eye = (lane == sub + start).astype(F32)
        tops = [work[m, start:stop, :] for m in mats]
        cols = [
            [jnp.broadcast_to(top[:, start + k : start + k + 1], shape) for k in range(PANEL)]
            for top in tops
        ]
        both = [jnp.where(in_panel, eye, top) for top in tops]
        for j in range(PANEL):
            for t in range(len(mats)):
                scale = lax.rsqrt(row(cols[t][j], j))
                low = cols[t][j] * scale
                below = jnp.where(sub > j, low, 0.0)
                for k in range(j + 1, PANEL):
                    cols[t][k] = cols[t][k] - below * row(low, k)
                pivot = row(tops[t], j) * scale
                tops[t] = jnp.where(sub == j, pivot, tops[t] - below * pivot)
                pivot = row(both[t], j) * scale
                both[t] = jnp.where(sub == j, pivot, both[t] - below * pivot)
        for t, m in enumerate(mats):
            upper[m, start:stop, :] = jnp.where(lane >= sub + start, tops[t], 0.0)
            inverse[m, start:stop, :] = jnp.where(lane < stop, both[t], 0.0)
            if stop < size:
                high, mid, low = split3(both[t])
                left = jnp.concatenate([high, high, mid, mid, high, low], axis=0)
                right = jnp.concatenate([high, mid, high, mid, low, high], axis=0)
                update = lax.dot_general(
                    left.astype(BF16), right.astype(BF16), (((0,), (0,)), ((), ())),
                    preferred_element_type=F32,
                )
                rest = lax.broadcasted_iota(jnp.int32, (size - stop, size), 1)
                drop = (rest >= start) & (rest < stop)
                old = jnp.where(drop, 0.0, work[m, stop:, :])
                work[m, stop:, :] = old - update[stop:, :]


def start_all(moves, sems, first=0):
    copies = [
        pltpu.make_async_copy(source, target, sems.at[first + i])
        for i, (source, target) in enumerate(moves)
    ]
    for copy in copies:
        copy.start()
    return copies


def wait_all(copies):
    for copy in copies:
        copy.wait()


def gram_kernel(rep, basis, trans, parts, grams, sent, lead, tail, rows, factors, sems):
    me = rep[0]
    leaves = basis.shape[0]
    came = start_all([(basis.at[i], rows.at[i]) for i in range(leaves)], sems)
    ready = start_all([(trans, factors)], sems, leaves)
    cut = start_all(
        [
            (parts.at[me ^ flip, which], out.at[at])
            for which, (out, flips) in enumerate(((lead, (1, 3)), (tail, (2, 3))))
            for at, flip in enumerate(flips)
        ],
        sems, leaves + 1,
    )
    for i in range(leaves):
        came[i].wait()
        grams[i] = lax.dot_general(
            rows[i], rows[i], (((0,), (0,)), ((), ())), preferred_element_type=F32
        ) * (1.0 / PTS)
    wait_all(ready)
    base, count = 0, leaves
    while count > 1:
        for pair in range(count // 2):
            one, two = base + 2 * pair, base + 2 * pair + 1
            grams[base + count + pair] = congruence(grams[one], factors[one]) + congruence(
                grams[two], factors[two]
            )
        base, count = base + count, count // 2
    sent[...] = congruence(grams[base], factors[base])
    wait_all(cut)


def factor_kernel(
    rep, grams, own, near, far_a, far_b, trans_top, packed, upper, inverse, work
):
    slots = grams.shape[0]
    size = grams.shape[1]
    high = rep[0] // 2
    mine = own[...] + near[...]
    other = far_a[...] + far_b[...]
    three_a = jnp.where(high == 0, mine, other)
    three_b = jnp.where(high == 0, other, mine)
    work[:slots] = grams[...]
    work[slots] = three_a
    work[slots + 1] = three_b
    work[slots + 2] = congruence(three_a, trans_top[0]) + congruence(three_b, trans_top[1])
    factorize(work, upper, inverse, list(range(slots + 3)))
    sub = lax.broadcasted_iota(jnp.int32, (size, size), 0)
    lane = lax.broadcasted_iota(jnp.int32, (size, size), 1)
    pairs = (slots + 1) // 2
    for even in range(0, slots, 2):
        square = upper[even]
        if even + 1 < slots:
            odd = upper[even + 1]
            square = jnp.where(lane >= sub, square, odd.T)
            diagonal = jnp.sum(jnp.where(lane == sub, odd, 0.0), axis=0, keepdims=True)
            at = pairs * size + even // 2 * TILE
            packed[at : at + TILE, :] = jnp.broadcast_to(diagonal, (TILE, size)).astype(BF16)
        at = even // 2 * size
        packed[at : at + size, :] = square.astype(BF16)


def finish_kernel(
    rep, basis, trans, trans_top, upper, inverse, orth, fresh, pool, top, four,
    rows, factors, orth_held, fresh_held, sems,
):
    leaves, slots = basis.shape[0], trans.shape[0]
    came = start_all([(trans, factors), (basis, rows)], sems)
    pool[...] = upper[:slots].astype(BF16)
    came[0].wait()
    gone = []
    base, count = 0, leaves
    while count > 1:
        for child in range(count):
            node = base + child
            fresh_held[node] = dot_nt(
                dot_nn(upper[node], factors[node]), inverse[base + count + child // 2]
            )
        base, count = base + count, count // 2
    three = base + 1
    own_three = inverse[three + rep[0] // 2]
    fresh_held[base] = dot_nt(dot_nn(upper[base], factors[base]), own_three)
    gone += start_all([(fresh_held, fresh)], sems, 2)
    came[1].wait()
    for i in range(leaves):
        orth_held[i] = lax.dot_general(
            rows[i], inverse[i].astype(BF16), (((1,), (1,)), ((), ())),
            preferred_element_type=F32,
        ).astype(BF16)
        gone += start_all([(orth_held.at[i], orth.at[i])], sems, 3 + i)
    share = four.shape[1]
    part = pl.ds(pl.multiple_of(rep[0] * share, share), share)
    for c in range(2):
        top[c] = dot_nt(dot_nn(upper[three + c, part, :], trans_top[c]), inverse[three + 2])
    four[0] = upper[three + 2, part, :]
    wait_all(gone)


def fold_kernel(rep, parts, lead, tail, lead_sum, tail_sum, kept, own, sems):
    me = rep[0]
    ready = start_all(
        [
            (parts.at[me ^ flip, which], own.at[at, which])
            for at, flips in enumerate(((2, 1), (0, 0)))
            for which, flip in enumerate(flips)
        ],
        sems,
    )
    for which, (came, out) in enumerate(((lead, lead_sum), (tail, tail_sum))):
        ready[which].wait()
        out[...] = (came[1].astype(F32) + own[0, which].astype(F32)).astype(BF16)
    for which, came in enumerate((lead, tail)):
        ready[2 + which].wait()
        kept[which] = (came[0].astype(F32) + own[1, which].astype(F32)).astype(BF16)


def half_kernel(row_slot, kept, lead_rest, tail_rest, pool, half):
    tiles = lead_rest.shape[0]
    for which, rest in enumerate((lead_rest, tail_rest)):
        for i in range(tiles):
            total = kept[which, i].astype(F32) + rest[i].astype(F32)
            k = which * tiles + i
            half[k] = jnp.dot(
                pool[row_slot[k]], total.astype(BF16), preferred_element_type=F32
            ).astype(BF16)


def project_kernel(slots, mine, col_node, half, *refs):
    count = 2 * REACH + 1
    pieces, (out, pool, sem) = refs[:count], refs[count:]
    rows = pieces[0].shape[0]
    size = out.shape[1]
    copies = [
        pltpu.make_async_copy(piece, pool.at[pl.ds(i * rows, rows)], sem.at[i])
        for i, piece in enumerate(pieces)
    ]
    for copy in copies:
        copy.start()
    sub = lax.broadcasted_iota(jnp.int32, (size, size), 0)
    lane = lax.broadcasted_iota(jnp.int32, (size, size), 1)
    above = (lane >= sub).astype(F32).astype(BF16)
    below = (lane < sub).astype(F32).astype(BF16)
    eye = (lane == sub).astype(F32).astype(BF16)
    pairs = (slots + 1) // 2
    for copy in copies:
        copy.wait()
    for k in range(out.shape[0]):
        piece, slot = col_node[k] // slots - mine[0] + REACH, col_node[k] % slots
        base = piece * rows
        square = pool[pl.ds(pl.multiple_of(base + slot // 2 * size, TILE), size), :]
        spot = jnp.minimum(slot // 2, slots // 2 - 1)
        at = pl.multiple_of(base + pairs * size + spot * TILE, TILE)
        diagonal = jnp.concatenate([pool[pl.ds(at, TILE), :]] * (size // TILE), axis=0)
        even = lax.dot_general(
            half[k], square * above, (((1,), (1,)), ((), ())), preferred_element_type=F32
        )
        odd = jnp.dot(half[k], square * below + diagonal * eye, preferred_element_type=F32)
        out[k] = jnp.where(slot % 2 == 0, even, odd).astype(BF16)


def shifted(value, steps):
    count = lax.axis_size(ALL)
    return lax.ppermute(value, ALL, [(i, (i + steps) % count) for i in range(count)])


def swapped(value, flip):
    return lax.ppermute(value, "rep", [(i, i ^ flip) for i in range(lax.axis_size("rep"))])


def per_device(leaf_basis, transfer, transfer_top, coupling_parts, row_slot, col_node):
    rank = transfer.shape[1]
    slots = transfer.shape[0]
    leaves = leaf_basis.shape[0]
    reps = lax.axis_size("rep")
    tiles = row_slot.shape[0]
    square = (rank, rank)
    rep = lax.axis_index("rep").astype(jnp.int32).reshape(1)

    parts = coupling_parts.reshape(reps, 2, tiles // 2, rank, rank)
    pair = jax.ShapeDtypeStruct((2, tiles // 2, *square), BF16)
    single = jax.ShapeDtypeStruct((tiles // 2, *square), BF16)
    leaf_basis, transfer, parts = (
        pltpu.with_memory_space_constraint(value, pltpu.HBM)
        for value in (leaf_basis, transfer, parts)
    )
    grams, sent, lead_out, tail_out = pl.pallas_call(
        gram_kernel,
        out_shape=[
            jax.ShapeDtypeStruct((slots, *square), F32),
            jax.ShapeDtypeStruct(square, F32),
            pair,
            pair,
        ],
        in_specs=[SMEM] + [ANY] * 3,
        out_specs=[VMEM] * 4,
        scratch_shapes=[
            pltpu.VMEM(leaf_basis.shape, BF16),
            pltpu.VMEM(transfer.shape, F32),
            pltpu.SemaphoreType.DMA((leaves + 5,)),
        ],
        compiler_params=PARAMS,
        name="grams",
    )(rep, leaf_basis, transfer, parts)
    near, far_a, far_b = (swapped(sent, flip) for flip in (1, 2, 3))
    lead = swapped(lead_out, 1)
    tail = swapped(tail_out, 2)
    lead_sum, tail_sum, kept = pl.pallas_call(
        fold_kernel,
        out_shape=[single, single, pair],
        in_specs=[SMEM, ANY, VMEM, VMEM],
        out_specs=[VMEM] * 3,
        scratch_shapes=[
            pltpu.VMEM((2, *pair.shape), BF16),
            pltpu.SemaphoreType.DMA((4,)),
        ],
        compiler_params=PARAMS,
        name="fold",
    )(rep, parts, lead, tail)
    lead_rest = swapped(lead_sum, 2)
    tail_rest = swapped(tail_sum, 1)
    pairs = (slots + 1) // 2
    nodes = (slots + 3, *square)
    packed, upper, inverse = pl.pallas_call(
        factor_kernel,
        out_shape=[
            jax.ShapeDtypeStruct((pairs * rank + slots // 2 * TILE, rank), BF16),
            jax.ShapeDtypeStruct(nodes, F32),
            jax.ShapeDtypeStruct(nodes, F32),
        ],
        in_specs=[SMEM] + [VMEM] * 6,
        out_specs=[VMEM] * 3,
        scratch_shapes=[pltpu.VMEM(nodes, F32)],
        compiler_params=PARAMS,
        name="factor",
    )(rep, grams, sent, near, far_a, far_b, transfer_top)
    pieces = [
        packed if offset == 0 else shifted(packed, -offset)
        for offset in range(-REACH, REACH + 1)
    ]
    share = rank // reps
    orth, fresh, pool, top, four = pl.pallas_call(
        finish_kernel,
        out_shape=[
            jax.ShapeDtypeStruct(leaf_basis.shape, BF16),
            jax.ShapeDtypeStruct(transfer.shape, F32),
            jax.ShapeDtypeStruct((slots, *square), BF16),
            jax.ShapeDtypeStruct((2, share, rank), F32),
            jax.ShapeDtypeStruct((1, share, rank), F32),
        ],
        in_specs=[SMEM, ANY, ANY, VMEM, VMEM, VMEM],
        out_specs=[ANY, ANY, VMEM, VMEM, VMEM],
        scratch_shapes=[
            pltpu.VMEM(leaf_basis.shape, BF16),
            pltpu.VMEM(transfer.shape, F32),
            pltpu.VMEM(leaf_basis.shape, BF16),
            pltpu.VMEM(transfer.shape, F32),
            pltpu.SemaphoreType.DMA((3 + leaves,)),
        ],
        compiler_params=PARAMS,
        name="finish",
    )(rep, leaf_basis, transfer, transfer_top, upper, inverse)
    half = pl.pallas_call(
        half_kernel,
        out_shape=jax.ShapeDtypeStruct((tiles, *square), BF16),
        in_specs=[SMEM] + [VMEM] * 4,
        out_specs=VMEM,
        compiler_params=PARAMS,
        name="half",
    )(row_slot, kept, lead_rest, tail_rest, pool)
    mine = lax.axis_index(ALL).astype(jnp.int32).reshape(1)
    projected = pl.pallas_call(
        functools.partial(project_kernel, slots),
        out_shape=jax.ShapeDtypeStruct((tiles, *square), BF16),
        in_specs=[SMEM, SMEM, VMEM] + [ANY] * (2 * REACH + 1),
        out_specs=VMEM,
        scratch_shapes=[
            pltpu.VMEM(((2 * REACH + 1) * packed.shape[0], rank), BF16),
            pltpu.SemaphoreType.DMA((2 * REACH + 1,)),
        ],
        compiler_params=PARAMS,
        name="project",
    )(mine, col_node, half, *pieces)
    return (orth, fresh, top, four, projected)


def solution(mesh):
    return jax.shard_map(
        per_device,
        mesh=mesh,
        in_specs=(
            P(ALL, None, None),
            P(ALL, None, None),
            P(("leaf", "dom"), None, None),
            P("rep", ("leaf", "dom"), None, None),
            P(ALL),
            P(ALL),
        ),
        out_specs=(
            P(ALL, None, None),
            P(ALL, None, None),
            P(("leaf", "dom"), "rep", None),
            P(("leaf", "dom"), "rep", None),
            P(ALL, None, None),
        ),
        check_vma=False,
    )
```

```python
import functools

import jax
import jax.numpy as jnp
from jax import lax
from jax.experimental import pallas as pl
from jax.experimental.pallas import tpu as pltpu
from jax.sharding import PartitionSpec as P


PTS = 512
REACH = 2
PANEL = 8
TILE = 16
ALL = ("leaf", "dom", "rep")
F32 = jnp.float32
BF16 = jnp.bfloat16
VMEM = pl.BlockSpec(memory_space=pltpu.VMEM)
SMEM = pl.BlockSpec(memory_space=pltpu.SMEM)
ANY = pl.BlockSpec(memory_space=pl.ANY)
PARAMS = pltpu.CompilerParams(vmem_limit_bytes=16 * 1024 * 1024)


def dot_nn(a, b):
    return lax.dot_general(
        a, b, (((1,), (0,)), ((), ())),
        precision=lax.Precision.HIGHEST, preferred_element_type=F32,
    )


def dot_tn(a, b):
    return lax.dot_general(
        a, b, (((0,), (0,)), ((), ())),
        precision=lax.Precision.HIGHEST, preferred_element_type=F32,
    )


def dot_nt(a, b):
    return lax.dot_general(
        a, b, (((1,), (1,)), ((), ())),
        precision=lax.Precision.HIGHEST, preferred_element_type=F32,
    )


def congruence(gram, trans):
    return dot_tn(trans, dot_nn(gram, trans))


def split3(x):
    high = x.astype(BF16).astype(F32)
    rest = x - high
    mid = rest.astype(BF16).astype(F32)
    return high, mid, rest - mid


def factorize(work, joint, mats):
    size = work.shape[-1]
    shape = (PANEL, size)
    sub = lax.broadcasted_iota(jnp.int32, shape, 0)
    lane = lax.broadcasted_iota(jnp.int32, shape, 1)

    def row(value, at):
        return jnp.broadcast_to(value[at : at + 1, :], shape)

    for start in range(0, size, PANEL):
        stop = start + PANEL
        in_panel = (lane >= start) & (lane < stop)
        eye = (lane == sub + start).astype(F32)
        tops = [work[m, start:stop, :] for m in mats]
        cols = [
            [jnp.broadcast_to(top[:, start + k : start + k + 1], shape) for k in range(PANEL)]
            for top in tops
        ]
        both = [jnp.where(in_panel, eye, top) for top in tops]
        for j in range(PANEL):
            for t in range(len(mats)):
                scale = lax.rsqrt(row(cols[t][j], j))
                low = cols[t][j] * scale
                below = jnp.where(sub > j, low, 0.0)
                for k in range(j + 1, PANEL):
                    cols[t][k] = cols[t][k] - below * row(low, k)
                pivot = row(tops[t], j) * scale
                tops[t] = jnp.where(sub == j, pivot, tops[t] - below * pivot)
                pivot = row(both[t], j) * scale
                both[t] = jnp.where(sub == j, pivot, both[t] - below * pivot)
        for t, m in enumerate(mats):
            joint[m, start:stop, :] = jnp.where(lane >= sub + start, tops[t], both[t])
            if stop < size:
                high, mid, low = split3(both[t])
                left = jnp.concatenate([high, high, mid, mid, high, low], axis=0)
                right = jnp.concatenate([high, mid, high, mid, low, high], axis=0)
                update = lax.dot_general(
                    left.astype(BF16), right.astype(BF16), (((0,), (0,)), ((), ())),
                    preferred_element_type=F32,
                )
                rest = lax.broadcasted_iota(jnp.int32, (size - stop, size), 1)
                drop = (rest >= start) & (rest < stop)
                old = jnp.where(drop, 0.0, work[m, stop:, :])
                work[m, stop:, :] = old - update[stop:, :]


def start_all(moves, sems, first=0):
    copies = [
        pltpu.make_async_copy(source, target, sems.at[first + i])
        for i, (source, target) in enumerate(moves)
    ]
    for copy in copies:
        copy.start()
    return copies


def wait_all(copies):
    for copy in copies:
        copy.wait()


def gram_kernel(rep, basis, trans, parts, grams, sent, lead, tail, add, rows, factors, sems):
    me = rep[0]
    leaves = basis.shape[0]
    came = start_all([(basis.at[i], rows.at[i]) for i in range(leaves)], sems)
    ready = start_all([(trans, factors)], sems, leaves)
    cut = start_all(
        [
            (parts.at[me ^ flip, which], out.at[at])
            for which, (out, flips) in enumerate(((lead, (1, 3)), (tail, (2, 3))))
            for at, flip in enumerate(flips)
        ],
        sems, leaves + 1,
    )
    cut += start_all(
        [(parts.at[me ^ 2, 0], add.at[0]), (parts.at[me ^ 1, 1], add.at[1])], sems, leaves + 5
    )
    for i in range(leaves):
        came[i].wait()
        grams[i] = lax.dot_general(
            rows[i], rows[i], (((0,), (0,)), ((), ())), preferred_element_type=F32
        ) * (1.0 / PTS)
    wait_all(ready)
    base, count = 0, leaves
    while count > 1:
        for pair in range(count // 2):
            one, two = base + 2 * pair, base + 2 * pair + 1
            grams[base + count + pair] = congruence(grams[one], factors[one]) + congruence(
                grams[two], factors[two]
            )
        base, count = base + count, count // 2
    sent[...] = congruence(grams[base], factors[base])
    wait_all(cut)


def factor_kernel(
    rep, grams, own, near, far_a, far_b, trans_top, packed, joint, work
):
    slots = grams.shape[0]
    size = grams.shape[1]
    high = rep[0] // 2
    mine = own[...] + near[...]
    other = far_a[...] + far_b[...]
    three_a = jnp.where(high == 0, mine, other)
    three_b = jnp.where(high == 0, other, mine)
    work[:slots] = grams[...]
    work[slots] = three_a
    work[slots + 1] = three_b
    work[slots + 2] = congruence(three_a, trans_top[0]) + congruence(three_b, trans_top[1])
    factorize(work, joint, list(range(slots + 3)))
    sub = lax.broadcasted_iota(jnp.int32, (size, size), 0)
    lane = lax.broadcasted_iota(jnp.int32, (size, size), 1)
    pairs = (slots + 1) // 2
    tile_row = lax.broadcasted_iota(jnp.int32, (TILE, size), 0)
    diagonals = jnp.zeros((TILE, size), F32)
    for even in range(0, slots, 2):
        square = joint[even]
        if even + 1 < slots:
            odd = joint[even + 1]
            square = jnp.where(lane >= sub, square, odd.T)
            diagonal = jnp.sum(jnp.where(lane == sub, odd, 0.0), axis=0, keepdims=True)
            diagonals = jnp.where(tile_row == even // 2, diagonal, diagonals)
        else:
            square = jnp.where(lane >= sub, square, 0.0)
        at = even // 2 * size
        packed[at : at + size, :] = square.astype(BF16)
    packed[pairs * size :, :] = diagonals.astype(BF16)


def finish_kernel(
    rep, basis, trans, trans_top, joint, parts, orth, fresh, pool, top, four, own,
    rows, factors, upper, inverse, orth_held, fresh_held, sems,
):
    leaves, slots = basis.shape[0], trans.shape[0]
    came = start_all([(trans, factors), (basis, rows)], sems)
    late = start_all([(parts.at[rep[0]], own)], sems, 3 + leaves)
    square = joint.shape[1:]
    sub = lax.broadcasted_iota(jnp.int32, square, 0)
    lane = lax.broadcasted_iota(jnp.int32, square, 1)
    for node in range(joint.shape[0]):
        both = joint[node]
        upper[node] = jnp.where(lane >= sub, both, 0.0)
        inverse[node] = jnp.where(lane < sub, both, jnp.where(lane == sub, 1.0 / both, 0.0))
    pool[...] = upper[:slots].astype(BF16)
    came[0].wait()
    gone = []
    base, count = 0, leaves
    while count > 1:
        for child in range(count):
            node = base + child
            fresh_held[node] = dot_nt(
                dot_nn(upper[node], factors[node]), inverse[base + count + child // 2]
            )
        base, count = base + count, count // 2
    three = base + 1
    own_three = inverse[three + rep[0] // 2]
    fresh_held[base] = dot_nt(dot_nn(upper[base], factors[base]), own_three)
    gone += start_all([(fresh_held, fresh)], sems, 2)
    came[1].wait()
    for i in range(leaves):
        orth_held[i] = lax.dot_general(
            rows[i], inverse[i].astype(BF16), (((1,), (1,)), ((), ())),
            preferred_element_type=F32,
        ).astype(BF16)
        gone += start_all([(orth_held.at[i], orth.at[i])], sems, 3 + i)
    share = four.shape[1]
    part = pl.ds(pl.multiple_of(rep[0] * share, share), share)
    for c in range(2):
        top[c] = dot_nt(dot_nn(upper[three + c, part, :], trans_top[c]), inverse[three + 2])
    four[0] = upper[three + 2, part, :]
    wait_all(gone + late)


def fold_kernel(add, lead, tail, lead_sum, tail_sum, kept):
    for which, (came, out) in enumerate(((lead, lead_sum), (tail, tail_sum))):
        out[...] = (came[1].astype(F32) + add[which].astype(F32)).astype(BF16)
        kept[which] = came[0]


def half_kernel(row_slot, own, kept, lead_rest, tail_rest, pool, half):
    tiles = lead_rest.shape[0]
    for which, rest in enumerate((lead_rest, tail_rest)):
        for i in range(tiles):
            total = (
                own[which, i].astype(F32) + kept[which, i].astype(F32) + rest[i].astype(F32)
            )
            k = which * tiles + i
            half[k] = jnp.dot(
                pool[row_slot[k]], total.astype(BF16), preferred_element_type=F32
            ).astype(BF16)


def project_kernel(slots, mine, col_node, half, *refs):
    count = 2 * REACH + 1
    pieces, (out, pool, held, sems) = refs[:count], refs[count:]
    rows = pieces[0].shape[0]
    size = out.shape[1]
    for i, piece in enumerate(pieces):
        pool[i * rows : (i + 1) * rows, :] = piece[...]
    sub = lax.broadcasted_iota(jnp.int32, (size, size), 0)
    lane = lax.broadcasted_iota(jnp.int32, (size, size), 1)
    tile_row = lax.broadcasted_iota(jnp.int32, (TILE, size), 0)
    above = (lane >= sub).astype(F32).astype(BF16)
    below = (lane < sub).astype(F32).astype(BF16)
    eye = (lane == sub).astype(F32).astype(BF16)
    pairs = (slots + 1) // 2
    gone = []
    for k in range(out.shape[0]):
        piece, slot = col_node[k] // slots - mine[0] + REACH, col_node[k] % slots
        base = piece * rows
        square = pool[pl.ds(pl.multiple_of(base + slot // 2 * size, TILE), size), :]
        tile = pool[pl.ds(pl.multiple_of(base + pairs * size, TILE), TILE), :].astype(F32)
        diagonal = jnp.sum(jnp.where(tile_row == slot // 2, tile, 0.0), axis=0, keepdims=True)
        spread = jnp.broadcast_to(diagonal, (size, size)).astype(BF16)
        even = lax.dot_general(
            half[k], square * above, (((1,), (1,)), ((), ())), preferred_element_type=F32
        )
        odd = jnp.dot(half[k], square * below + spread * eye, preferred_element_type=F32)
        held[k] = jnp.where(slot % 2 == 0, even, odd).astype(BF16)
        if k % 4 == 3:
            gone += start_all([(held.at[k - 3 : k + 1], out.at[k - 3 : k + 1])], sems, k // 4)
    wait_all(gone)


def shifted(value, steps):
    count = lax.axis_size(ALL)
    return lax.ppermute(value, ALL, [(i, (i + steps) % count) for i in range(count)])


def swapped(value, flip):
    return lax.ppermute(value, "rep", [(i, i ^ flip) for i in range(lax.axis_size("rep"))])


def per_device(leaf_basis, transfer, transfer_top, coupling_parts, row_slot, col_node):
    rank = transfer.shape[1]
    slots = transfer.shape[0]
    leaves = leaf_basis.shape[0]
    reps = lax.axis_size("rep")
    tiles = row_slot.shape[0]
    square = (rank, rank)
    rep = lax.axis_index("rep").astype(jnp.int32).reshape(1)

    parts = coupling_parts.reshape(reps, 2, tiles // 2, rank, rank)
    pair = jax.ShapeDtypeStruct((2, tiles // 2, *square), BF16)
    single = jax.ShapeDtypeStruct((tiles // 2, *square), BF16)
    leaf_basis, transfer, parts = (
        pltpu.with_memory_space_constraint(value, pltpu.HBM)
        for value in (leaf_basis, transfer, parts)
    )
    grams, sent, lead_out, tail_out, add = pl.pallas_call(
        gram_kernel,
        out_shape=[
            jax.ShapeDtypeStruct((slots, *square), F32),
            jax.ShapeDtypeStruct(square, F32),
            pair,
            pair,
            pair,
        ],
        in_specs=[SMEM] + [ANY] * 3,
        out_specs=[VMEM] * 5,
        scratch_shapes=[
            pltpu.VMEM(leaf_basis.shape, BF16),
            pltpu.VMEM(transfer.shape, F32),
            pltpu.SemaphoreType.DMA((leaves + 7,)),
        ],
        compiler_params=PARAMS,
        name="grams",
    )(rep, leaf_basis, transfer, parts)
    far_b = swapped(sent, 3)
    near, far_a = swapped(sent, 1), swapped(sent, 2)
    lead = swapped(lead_out, 1)
    tail = swapped(tail_out, 2)
    pairs = (slots + 1) // 2
    nodes = (slots + 3, *square)
    packed, joint = pl.pallas_call(
        factor_kernel,
        out_shape=[
            jax.ShapeDtypeStruct((pairs * rank + TILE, rank), BF16),
            jax.ShapeDtypeStruct(nodes, F32),
        ],
        in_specs=[SMEM] + [VMEM] * 6,
        out_specs=[VMEM] * 2,
        scratch_shapes=[pltpu.VMEM(nodes, F32)],
        compiler_params=PARAMS,
        name="factor",
    )(rep, grams, sent, near, far_a, far_b, transfer_top)
    lead_sum, tail_sum, kept = pl.pallas_call(
        fold_kernel,
        out_shape=[single, single, pair],
        in_specs=[VMEM] * 3,
        out_specs=[VMEM] * 3,
        compiler_params=PARAMS,
        name="fold",
    )(add, lead, tail)
    lead_rest = swapped(lead_sum, 2)
    tail_rest = swapped(tail_sum, 1)
    pieces = [
        packed if offset == 0 else shifted(packed, -offset)
        for offset in range(-REACH, REACH + 1)
    ]
    share = rank // reps
    orth, fresh, pool, top, four, own = pl.pallas_call(
        finish_kernel,
        out_shape=[
            jax.ShapeDtypeStruct(leaf_basis.shape, BF16),
            jax.ShapeDtypeStruct(transfer.shape, F32),
            jax.ShapeDtypeStruct((slots, *square), BF16),
            jax.ShapeDtypeStruct((2, share, rank), F32),
            jax.ShapeDtypeStruct((1, share, rank), F32),
            pair,
        ],
        in_specs=[SMEM, ANY, ANY, VMEM, VMEM, ANY],
        out_specs=[ANY, ANY, VMEM, VMEM, VMEM, VMEM],
        scratch_shapes=[
            pltpu.VMEM(leaf_basis.shape, BF16),
            pltpu.VMEM(transfer.shape, F32),
            pltpu.VMEM(nodes, F32),
            pltpu.VMEM(nodes, F32),
            pltpu.VMEM(leaf_basis.shape, BF16),
            pltpu.VMEM(transfer.shape, F32),
            pltpu.SemaphoreType.DMA((4 + leaves,)),
        ],
        compiler_params=PARAMS,
        name="finish",
    )(rep, leaf_basis, transfer, transfer_top, joint, parts)
    half = pl.pallas_call(
        half_kernel,
        out_shape=jax.ShapeDtypeStruct((tiles, *square), BF16),
        in_specs=[SMEM] + [VMEM] * 5,
        out_specs=VMEM,
        compiler_params=PARAMS,
        name="half",
    )(row_slot, own, kept, lead_rest, tail_rest, pool)
    mine = lax.axis_index(ALL).astype(jnp.int32).reshape(1)
    projected = pl.pallas_call(
        functools.partial(project_kernel, slots),
        out_shape=jax.ShapeDtypeStruct((tiles, *square), BF16),
        in_specs=[SMEM, SMEM, VMEM] + [VMEM] * (2 * REACH + 1),
        out_specs=ANY,
        scratch_shapes=[
            pltpu.VMEM(((2 * REACH + 1) * packed.shape[0], rank), BF16),
            pltpu.VMEM((tiles, *square), BF16),
            pltpu.SemaphoreType.DMA((tiles // 4,)),
        ],
        compiler_params=PARAMS,
        name="project",
    )(mine, col_node, half, *pieces)
    return (orth, fresh, top, four, projected)


def solution(mesh):
    return jax.shard_map(
        per_device,
        mesh=mesh,
        in_specs=(
            P(ALL, None, None),
            P(ALL, None, None),
            P(("leaf", "dom"), None, None),
            P("rep", ("leaf", "dom"), None, None),
            P(ALL),
            P(ALL),
        ),
        out_specs=(
            P(ALL, None, None),
            P(ALL, None, None),
            P(("leaf", "dom"), "rep", None),
            P(("leaf", "dom"), "rep", None),
            P(ALL, None, None),
        ),
        check_vma=False,
    )
```

```python
import functools

import jax
import jax.numpy as jnp
from jax import lax
from jax.experimental import pallas as pl
from jax.experimental.pallas import tpu as pltpu
from jax.sharding import PartitionSpec as P


PTS = 512
REACH = 2
PANEL = 8
TILE = 16
ALL = ("leaf", "dom", "rep")
F32 = jnp.float32
BF16 = jnp.bfloat16
VMEM = pl.BlockSpec(memory_space=pltpu.VMEM)
SMEM = pl.BlockSpec(memory_space=pltpu.SMEM)
ANY = pl.BlockSpec(memory_space=pl.ANY)
PARAMS = pltpu.CompilerParams(vmem_limit_bytes=16 * 1024 * 1024)


def dot_nn(a, b):
    return lax.dot_general(
        a, b, (((1,), (0,)), ((), ())),
        precision=lax.Precision.HIGHEST, preferred_element_type=F32,
    )


def dot_tn(a, b):
    return lax.dot_general(
        a, b, (((0,), (0,)), ((), ())),
        precision=lax.Precision.HIGHEST, preferred_element_type=F32,
    )


def dot_nt(a, b):
    return lax.dot_general(
        a, b, (((1,), (1,)), ((), ())),
        precision=lax.Precision.HIGHEST, preferred_element_type=F32,
    )


def congruence(gram, trans):
    return dot_tn(trans, dot_nn(gram, trans))


def split3(x):
    high = x.astype(BF16).astype(F32)
    rest = x - high
    mid = rest.astype(BF16).astype(F32)
    return high, mid, rest - mid


def factorize(work, joint, mats):
    size = work.shape[-1]
    shape = (PANEL, size)
    sub = lax.broadcasted_iota(jnp.int32, shape, 0)
    lane = lax.broadcasted_iota(jnp.int32, shape, 1)

    def row(value, at):
        return jnp.broadcast_to(value[at : at + 1, :], shape)

    for start in range(0, size, PANEL):
        stop = start + PANEL
        in_panel = (lane >= start) & (lane < stop)
        eye = (lane == sub + start).astype(F32)
        tops = [work[m, start:stop, :] for m in mats]
        cols = [
            [jnp.broadcast_to(top[:, start + k : start + k + 1], shape) for k in range(PANEL)]
            for top in tops
        ]
        both = [jnp.where(in_panel, eye, top) for top in tops]
        block = [jnp.zeros(shape, F32) for _ in mats]
        scales = [jnp.zeros(shape, F32) for _ in mats]
        for j in range(PANEL):
            for t in range(len(mats)):
                scale = lax.rsqrt(row(cols[t][j], j))
                scales[t] = jnp.where(sub == j, scale, scales[t])
                block[t] = jnp.where(lane == start + j, cols[t][j], block[t])
                low = cols[t][j] * scale
                below = jnp.where(sub > j, low, 0.0)
                for k in range(j + 1, PANEL):
                    cols[t][k] = cols[t][k] - below * row(low, k)
                pivot = row(both[t], j) * scale
                both[t] = jnp.where(sub == j, pivot, both[t] - below * pivot)
        upper = in_panel & (lane >= sub + start)
        for t, m in enumerate(mats):
            joint[m, start:stop, :] = jnp.where(upper, block[t] * scales[t], both[t])
            if stop < size:
                high, mid, low = split3(both[t])
                left = jnp.concatenate([high, high, mid, mid, high, low], axis=0)
                right = jnp.concatenate([high, mid, high, mid, low, high], axis=0)
                update = lax.dot_general(
                    left.astype(BF16), right.astype(BF16), (((0,), (0,)), ((), ())),
                    preferred_element_type=F32,
                )
                rest = lax.broadcasted_iota(jnp.int32, (size - stop, size), 1)
                drop = (rest >= start) & (rest < stop)
                old = jnp.where(drop, 0.0, work[m, stop:, :])
                work[m, stop:, :] = old - update[stop:, :]


def start_all(moves, sems, first=0):
    copies = [
        pltpu.make_async_copy(source, target, sems.at[first + i])
        for i, (source, target) in enumerate(moves)
    ]
    for copy in copies:
        copy.start()
    return copies


def wait_all(copies):
    for copy in copies:
        copy.wait()


def fold_symmetric(value):
    size = value.shape[0]
    block = size // 4
    lane = lax.broadcasted_iota(jnp.int32, (block, size), 1)
    last = pltpu.roll(value[3 * block :], block, 1)
    near = jnp.where(lane >= block, value[block : 2 * block], last)
    low = pltpu.roll(value[5 * block // 2 : 3 * block], 2 * block, 1)
    half = lane[: block // 2] >= 2 * block
    return value[:block], near, jnp.where(half, value[2 * block : 5 * block // 2], low)


def unfold_symmetric(rows):
    size = rows.shape[1]
    block = size // 4
    near, far = rows[block : 2 * block], rows[2 * block :]
    whole = jnp.concatenate(
        [rows[: 2 * block], far, pltpu.roll(far, 2 * block, 1), pltpu.roll(near, 3 * block, 1)],
        axis=0,
    )
    sub = lax.broadcasted_iota(jnp.int32, whole.shape, 0)
    lane = lax.broadcasted_iota(jnp.int32, whole.shape, 1)
    return jnp.where(lane >= sub, whole, whole.T)


def gram_kernel(rep, basis, trans, parts, grams, sent, lead, tail, add, rows, factors, sems):
    me = rep[0]
    leaves = basis.shape[0]
    came = start_all([(basis.at[i], rows.at[i]) for i in range(leaves)], sems)
    ready = start_all([(trans, factors)], sems, leaves)
    cut = start_all(
        [
            (parts.at[me ^ flip, which], out.at[at])
            for which, (out, flips) in enumerate(((lead, (1, 3)), (tail, (2, 3))))
            for at, flip in enumerate(flips)
        ],
        sems, leaves + 1,
    )
    cut += start_all(
        [(parts.at[me ^ 2, 0], add.at[0]), (parts.at[me ^ 1, 1], add.at[1])], sems, leaves + 5
    )
    for i in range(leaves):
        came[i].wait()
        grams[i] = lax.dot_general(
            rows[i], rows[i], (((0,), (0,)), ((), ())), preferred_element_type=F32
        ) * (1.0 / PTS)
    wait_all(ready)
    base, count = 0, leaves
    while count > 1:
        for pair in range(count // 2):
            one, two = base + 2 * pair, base + 2 * pair + 1
            grams[base + count + pair] = congruence(grams[one], factors[one]) + congruence(
                grams[two], factors[two]
            )
        base, count = base + count, count // 2
    at = 0
    for rows_of in fold_symmetric(congruence(grams[base], factors[base])):
        sent[at : at + rows_of.shape[0], :] = rows_of
        at += rows_of.shape[0]
    wait_all(cut)


def factor_kernel(
    rep, grams, own, near, far_a, far_b, trans_top, joint, work
):
    slots = grams.shape[0]
    high = rep[0] // 2
    mine = unfold_symmetric(own[...] + near[...])
    other = unfold_symmetric(far_a[...] + far_b[...])
    three_a = jnp.where(high == 0, mine, other)
    three_b = jnp.where(high == 0, other, mine)
    work[:slots] = grams[...]
    work[slots] = three_a
    work[slots + 1] = three_b
    work[slots + 2] = congruence(three_a, trans_top[0]) + congruence(three_b, trans_top[1])
    factorize(work, joint, list(range(slots + 3)))


def pack_kernel(slots, joint, packed):
    size = joint.shape[1]
    sub = lax.broadcasted_iota(jnp.int32, (size, size), 0)
    lane = lax.broadcasted_iota(jnp.int32, (size, size), 1)
    pairs = (slots + 1) // 2
    tile_row = lax.broadcasted_iota(jnp.int32, (TILE, size), 0)
    diagonals = jnp.zeros((TILE, size), F32)
    for even in range(0, slots, 2):
        square = joint[even]
        if even + 1 < slots:
            odd = joint[even + 1]
            square = jnp.where(lane >= sub, square, odd.T)
            diagonal = jnp.sum(jnp.where(lane == sub, odd, 0.0), axis=0, keepdims=True)
            diagonals = jnp.where(tile_row == even // 2, diagonal, diagonals)
        else:
            square = jnp.where(lane >= sub, square, 0.0)
        at = even // 2 * size
        packed[at : at + size, :] = square.astype(BF16)
    packed[pairs * size :, :] = diagonals.astype(BF16)


def finish_kernel(
    rep, basis, trans, trans_top, joint, parts, orth, fresh, pool, top, four, own,
    rows, factors, upper, inverse, orth_held, fresh_held, sems,
):
    leaves, slots = basis.shape[0], trans.shape[0]
    came = start_all([(trans, factors), (basis, rows)], sems)
    late = start_all([(parts.at[rep[0]], own)], sems, 3 + leaves)
    square = joint.shape[1:]
    sub = lax.broadcasted_iota(jnp.int32, square, 0)
    lane = lax.broadcasted_iota(jnp.int32, square, 1)
    for node in range(joint.shape[0]):
        both = joint[node]
        upper[node] = jnp.where(lane >= sub, both, 0.0)
        inverse[node] = jnp.where(lane < sub, both, jnp.where(lane == sub, 1.0 / both, 0.0))
    pool[...] = upper[:slots].astype(BF16)
    came[0].wait()
    gone = []
    base, count = 0, leaves
    while count > 1:
        for child in range(count):
            node = base + child
            fresh_held[node] = dot_nt(
                dot_nn(upper[node], factors[node]), inverse[base + count + child // 2]
            )
        base, count = base + count, count // 2
    three = base + 1
    own_three = inverse[three + rep[0] // 2]
    fresh_held[base] = dot_nt(dot_nn(upper[base], factors[base]), own_three)
    gone += start_all([(fresh_held, fresh)], sems, 2)
    came[1].wait()
    for i in range(leaves):
        orth_held[i] = lax.dot_general(
            rows[i], inverse[i].astype(BF16), (((1,), (1,)), ((), ())),
            preferred_element_type=F32,
        ).astype(BF16)
        gone += start_all([(orth_held.at[i], orth.at[i])], sems, 3 + i)
    share = four.shape[1]
    part = pl.ds(pl.multiple_of(rep[0] * share, share), share)
    for c in range(2):
        top[c] = dot_nt(dot_nn(upper[three + c, part, :], trans_top[c]), inverse[three + 2])
    four[0] = upper[three + 2, part, :]
    wait_all(gone + late)


def fold_kernel(add, lead, tail, lead_sum, tail_sum, kept):
    for which, (came, out) in enumerate(((lead, lead_sum), (tail, tail_sum))):
        out[...] = (came[1].astype(F32) + add[which].astype(F32)).astype(BF16)
        kept[which] = came[0]


def half_kernel(row_slot, own, kept, lead_rest, tail_rest, pool, half):
    tiles = lead_rest.shape[0]
    for which, rest in enumerate((lead_rest, tail_rest)):
        for i in range(tiles):
            total = (
                own[which, i].astype(F32) + kept[which, i].astype(F32) + rest[i].astype(F32)
            )
            k = which * tiles + i
            half[k] = jnp.dot(
                pool[row_slot[k]], total.astype(BF16), preferred_element_type=F32
            ).astype(BF16)


def project_kernel(slots, mine, col_node, half, *refs):
    count = 2 * REACH + 1
    pieces, (out, pool, held, sems) = refs[:count], refs[count:]
    rows = pieces[0].shape[0]
    size = out.shape[1]
    for i, piece in enumerate(pieces):
        pool[i * rows : (i + 1) * rows, :] = piece[...]
    sub = lax.broadcasted_iota(jnp.int32, (size, size), 0)
    lane = lax.broadcasted_iota(jnp.int32, (size, size), 1)
    tile_row = lax.broadcasted_iota(jnp.int32, (TILE, size), 0)
    above = (lane >= sub).astype(F32).astype(BF16)
    below = (lane < sub).astype(F32).astype(BF16)
    eye = (lane == sub).astype(F32).astype(BF16)
    pairs = (slots + 1) // 2
    gone = []
    for k in range(out.shape[0]):
        piece, slot = col_node[k] // slots - mine[0] + REACH, col_node[k] % slots
        base = piece * rows
        square = pool[pl.ds(pl.multiple_of(base + slot // 2 * size, TILE), size), :]
        tile = pool[pl.ds(pl.multiple_of(base + pairs * size, TILE), TILE), :].astype(F32)
        diagonal = jnp.sum(jnp.where(tile_row == slot // 2, tile, 0.0), axis=0, keepdims=True)
        spread = jnp.broadcast_to(diagonal, (size, size)).astype(BF16)
        even = lax.dot_general(
            half[k], square * above, (((1,), (1,)), ((), ())), preferred_element_type=F32
        )
        odd = jnp.dot(half[k], square * below + spread * eye, preferred_element_type=F32)
        held[k] = jnp.where(slot % 2 == 0, even, odd).astype(BF16)
        if k % 4 == 3:
            gone += start_all([(held.at[k - 3 : k + 1], out.at[k - 3 : k + 1])], sems, k // 4)
    wait_all(gone)


def shifted(value, steps):
    count = lax.axis_size(ALL)
    return lax.ppermute(value, ALL, [(i, (i + steps) % count) for i in range(count)])


def swapped(value, flip):
    return lax.ppermute(value, "rep", [(i, i ^ flip) for i in range(lax.axis_size("rep"))])


def per_device(leaf_basis, transfer, transfer_top, coupling_parts, row_slot, col_node):
    rank = transfer.shape[1]
    slots = transfer.shape[0]
    leaves = leaf_basis.shape[0]
    reps = lax.axis_size("rep")
    tiles = row_slot.shape[0]
    square = (rank, rank)
    rep = lax.axis_index("rep").astype(jnp.int32).reshape(1)

    parts = coupling_parts.reshape(reps, 2, tiles // 2, rank, rank)
    pair = jax.ShapeDtypeStruct((2, tiles // 2, *square), BF16)
    single = jax.ShapeDtypeStruct((tiles // 2, *square), BF16)
    leaf_basis, transfer, parts = (
        pltpu.with_memory_space_constraint(value, pltpu.HBM)
        for value in (leaf_basis, transfer, parts)
    )
    grams, sent, lead_out, tail_out, add = pl.pallas_call(
        gram_kernel,
        out_shape=[
            jax.ShapeDtypeStruct((slots, *square), F32),
            jax.ShapeDtypeStruct((5 * rank // 8, rank), F32),
            pair,
            pair,
            pair,
        ],
        in_specs=[SMEM] + [ANY] * 3,
        out_specs=[VMEM] * 5,
        scratch_shapes=[
            pltpu.VMEM(leaf_basis.shape, BF16),
            pltpu.VMEM(transfer.shape, F32),
            pltpu.SemaphoreType.DMA((leaves + 7,)),
        ],
        compiler_params=PARAMS,
        name="grams",
    )(rep, leaf_basis, transfer, parts)
    far_b = swapped(sent, 3)
    near, far_a = swapped(sent, 1), swapped(sent, 2)
    lead = swapped(lead_out, 1)
    tail = swapped(tail_out, 2)
    pairs = (slots + 1) // 2
    nodes = (slots + 3, *square)
    joint = pl.pallas_call(
        factor_kernel,
        out_shape=jax.ShapeDtypeStruct(nodes, F32),
        in_specs=[SMEM] + [VMEM] * 6,
        out_specs=VMEM,
        scratch_shapes=[pltpu.VMEM(nodes, F32)],
        compiler_params=PARAMS,
        name="factor",
    )(rep, grams, sent, near, far_a, far_b, transfer_top)
    lead_sum, tail_sum, kept = pl.pallas_call(
        fold_kernel,
        out_shape=[single, single, pair],
        in_specs=[VMEM] * 3,
        out_specs=[VMEM] * 3,
        compiler_params=PARAMS,
        name="fold",
    )(add, lead, tail)
    lead_rest = swapped(lead_sum, 2)
    tail_rest = swapped(tail_sum, 1)
    packed = pl.pallas_call(
        functools.partial(pack_kernel, slots),
        out_shape=jax.ShapeDtypeStruct((pairs * rank + TILE, rank), BF16),
        in_specs=[VMEM],
        out_specs=VMEM,
        compiler_params=PARAMS,
        name="pack",
    )(joint)
    pieces = [
        packed if offset == 0 else shifted(packed, -offset)
        for offset in range(-REACH, REACH + 1)
    ]
    share = rank // reps
    orth, fresh, pool, top, four, own = pl.pallas_call(
        finish_kernel,
        out_shape=[
            jax.ShapeDtypeStruct(leaf_basis.shape, BF16),
            jax.ShapeDtypeStruct(transfer.shape, F32),
            jax.ShapeDtypeStruct((slots, *square), BF16),
            jax.ShapeDtypeStruct((2, share, rank), F32),
            jax.ShapeDtypeStruct((1, share, rank), F32),
            pair,
        ],
        in_specs=[SMEM, ANY, ANY, VMEM, VMEM, ANY],
        out_specs=[ANY, ANY, VMEM, VMEM, VMEM, VMEM],
        scratch_shapes=[
            pltpu.VMEM(leaf_basis.shape, BF16),
            pltpu.VMEM(transfer.shape, F32),
            pltpu.VMEM(nodes, F32),
            pltpu.VMEM(nodes, F32),
            pltpu.VMEM(leaf_basis.shape, BF16),
            pltpu.VMEM(transfer.shape, F32),
            pltpu.SemaphoreType.DMA((4 + leaves,)),
        ],
        compiler_params=PARAMS,
        name="finish",
    )(rep, leaf_basis, transfer, transfer_top, joint, parts)
    half = pl.pallas_call(
        half_kernel,
        out_shape=jax.ShapeDtypeStruct((tiles, *square), BF16),
        in_specs=[SMEM] + [VMEM] * 5,
        out_specs=VMEM,
        compiler_params=PARAMS,
        name="half",
    )(row_slot, own, kept, lead_rest, tail_rest, pool)
    mine = lax.axis_index(ALL).astype(jnp.int32).reshape(1)
    projected = pl.pallas_call(
        functools.partial(project_kernel, slots),
        out_shape=jax.ShapeDtypeStruct((tiles, *square), BF16),
        in_specs=[SMEM, SMEM, VMEM] + [VMEM] * (2 * REACH + 1),
        out_specs=ANY,
        scratch_shapes=[
            pltpu.VMEM(((2 * REACH + 1) * packed.shape[0], rank), BF16),
            pltpu.VMEM((tiles, *square), BF16),
            pltpu.SemaphoreType.DMA((tiles // 4,)),
        ],
        compiler_params=PARAMS,
        name="project",
    )(mine, col_node, half, *pieces)
    return (orth, fresh, top, four, projected)


def solution(mesh):
    return jax.shard_map(
        per_device,
        mesh=mesh,
        in_specs=(
            P(ALL, None, None),
            P(ALL, None, None),
            P(("leaf", "dom"), None, None),
            P("rep", ("leaf", "dom"), None, None),
            P(ALL),
            P(ALL),
        ),
        out_specs=(
            P(ALL, None, None),
            P(ALL, None, None),
            P(("leaf", "dom"), "rep", None),
            P(("leaf", "dom"), "rep", None),
            P(ALL, None, None),
        ),
        check_vma=False,
    )
```

```python
import functools

import jax
import jax.numpy as jnp
from jax import lax
from jax.experimental import pallas as pl
from jax.experimental.pallas import tpu as pltpu
from jax.sharding import PartitionSpec as P


PTS = 512
REACH = 2
PANEL = 8
TILE = 16
ALL = ("leaf", "dom", "rep")
F32 = jnp.float32
BF16 = jnp.bfloat16
VMEM = pl.BlockSpec(memory_space=pltpu.VMEM)
SMEM = pl.BlockSpec(memory_space=pltpu.SMEM)
ANY = pl.BlockSpec(memory_space=pl.ANY)
PARAMS = pltpu.CompilerParams(vmem_limit_bytes=16 * 1024 * 1024)


def dot_nn(a, b):
    return lax.dot_general(
        a, b, (((1,), (0,)), ((), ())),
        precision=lax.Precision.HIGHEST, preferred_element_type=F32,
    )


def dot_tn(a, b):
    return lax.dot_general(
        a, b, (((0,), (0,)), ((), ())),
        precision=lax.Precision.HIGHEST, preferred_element_type=F32,
    )


def dot_nt(a, b):
    return lax.dot_general(
        a, b, (((1,), (1,)), ((), ())),
        precision=lax.Precision.HIGHEST, preferred_element_type=F32,
    )


def congruence(gram, trans):
    return dot_tn(trans, dot_nn(gram, trans))


def split3(x):
    high = x.astype(BF16).astype(F32)
    rest = x - high
    mid = rest.astype(BF16).astype(F32)
    return high, mid, rest - mid


def factorize(work, joint, mats):
    size = work.shape[-1]
    shape = (PANEL, size)
    sub = lax.broadcasted_iota(jnp.int32, shape, 0)
    lane = lax.broadcasted_iota(jnp.int32, shape, 1)

    def row(value, at):
        return jnp.broadcast_to(value[at : at + 1, :], shape)

    for start in range(0, size, PANEL):
        stop = start + PANEL
        in_panel = (lane >= start) & (lane < stop)
        eye = (lane == sub + start).astype(F32)
        tops = [work[m, start:stop, :] for m in mats]
        cols = [
            [jnp.broadcast_to(top[:, start + k : start + k + 1], shape) for k in range(PANEL)]
            for top in tops
        ]
        both = [jnp.where(in_panel, eye, top) for top in tops]
        block = [jnp.zeros(shape, F32) for _ in mats]
        scales = [jnp.zeros(shape, F32) for _ in mats]
        for j in range(PANEL):
            for t in range(len(mats)):
                scale = lax.rsqrt(row(cols[t][j], j))
                scales[t] = jnp.where(sub == j, scale, scales[t])
                block[t] = jnp.where(lane == start + j, cols[t][j], block[t])
                low = cols[t][j] * scale
                below = jnp.where(sub > j, low, 0.0)
                for k in range(j + 1, PANEL):
                    cols[t][k] = cols[t][k] - below * row(low, k)
                pivot = row(both[t], j) * scale
                both[t] = jnp.where(sub == j, pivot, both[t] - below * pivot)
        upper = in_panel & (lane >= sub + start)
        for t, m in enumerate(mats):
            joint[m, start:stop, :] = jnp.where(upper, block[t] * scales[t], both[t])
            if stop < size:
                high, mid, low = split3(both[t])
                left = jnp.concatenate([high, high, mid, mid, high, low], axis=0)
                right = jnp.concatenate([high, mid, high, mid, low, high], axis=0)
                update = lax.dot_general(
                    left.astype(BF16), right.astype(BF16), (((0,), (0,)), ((), ())),
                    preferred_element_type=F32,
                )
                rest = lax.broadcasted_iota(jnp.int32, (size - stop, size), 1)
                drop = (rest >= start) & (rest < stop)
                old = jnp.where(drop, 0.0, work[m, stop:, :])
                work[m, stop:, :] = old - update[stop:, :]


def start_all(moves, sems, first=0):
    copies = [
        pltpu.make_async_copy(source, target, sems.at[first + i])
        for i, (source, target) in enumerate(moves)
    ]
    for copy in copies:
        copy.start()
    return copies


def wait_all(copies):
    for copy in copies:
        copy.wait()


def fold_symmetric(value):
    size = value.shape[0]
    block = size // 4
    lane = lax.broadcasted_iota(jnp.int32, (block, size), 1)
    last = pltpu.roll(value[3 * block :], block, 1)
    near = jnp.where(lane >= block, value[block : 2 * block], last)
    low = pltpu.roll(value[5 * block // 2 : 3 * block], 2 * block, 1)
    half = lane[: block // 2] >= 2 * block
    return value[:block], near, jnp.where(half, value[2 * block : 5 * block // 2], low)


def unfold_symmetric(rows):
    size = rows.shape[1]
    block = size // 4
    near, far = rows[block : 2 * block], rows[2 * block :]
    whole = jnp.concatenate(
        [rows[: 2 * block], far, pltpu.roll(far, 2 * block, 1), pltpu.roll(near, 3 * block, 1)],
        axis=0,
    )
    sub = lax.broadcasted_iota(jnp.int32, whole.shape, 0)
    lane = lax.broadcasted_iota(jnp.int32, whole.shape, 1)
    return jnp.where(lane >= sub, whole, whole.T)


def gram_kernel(rep, basis, trans, parts, grams, sent, lead, tail, add, rows, factors, sems):
    me = rep[0]
    leaves = basis.shape[0]
    came = start_all([(basis.at[i], rows.at[i]) for i in range(leaves)], sems)
    ready = start_all([(trans, factors)], sems, leaves)
    cut = start_all(
        [
            (parts.at[me ^ flip, which], out.at[at])
            for which, (out, flips) in enumerate(((lead, (1, 3)), (tail, (2, 3))))
            for at, flip in enumerate(flips)
        ],
        sems, leaves + 1,
    )
    cut += start_all(
        [(parts.at[me ^ 2, 0], add.at[0]), (parts.at[me ^ 1, 1], add.at[1])], sems, leaves + 5
    )
    for i in range(leaves):
        came[i].wait()
        grams[i] = lax.dot_general(
            rows[i], rows[i], (((0,), (0,)), ((), ())), preferred_element_type=F32
        ) * (1.0 / PTS)
    wait_all(ready)
    base, count = 0, leaves
    while count > 1:
        for pair in range(count // 2):
            one, two = base + 2 * pair, base + 2 * pair + 1
            grams[base + count + pair] = congruence(grams[one], factors[one]) + congruence(
                grams[two], factors[two]
            )
        base, count = base + count, count // 2
    at = 0
    for rows_of in fold_symmetric(congruence(grams[base], factors[base])):
        sent[at : at + rows_of.shape[0], :] = rows_of
        at += rows_of.shape[0]
    wait_all(cut)


def factor_kernel(
    rep, grams, own, near, far_a, far_b, trans_top, joint, work
):
    slots = grams.shape[0]
    high = rep[0] // 2
    mine = unfold_symmetric(own[...] + near[...])
    other = unfold_symmetric(far_a[...] + far_b[...])
    three_a = jnp.where(high == 0, mine, other)
    three_b = jnp.where(high == 0, other, mine)
    work[:slots] = grams[...]
    work[slots] = three_a
    work[slots + 1] = three_b
    work[slots + 2] = congruence(three_a, trans_top[0]) + congruence(three_b, trans_top[1])
    factorize(work, joint, list(range(slots + 3)))


def pack_kernel(slots, joint, packed):
    size = joint.shape[1]
    sub = lax.broadcasted_iota(jnp.int32, (size, size), 0)
    lane = lax.broadcasted_iota(jnp.int32, (size, size), 1)
    pairs = (slots + 1) // 2
    tile_row = lax.broadcasted_iota(jnp.int32, (TILE, size), 0)
    diagonals = jnp.zeros((TILE, size), F32)
    for even in range(0, slots, 2):
        square = joint[even]
        if even + 1 < slots:
            odd = joint[even + 1]
            square = jnp.where(lane >= sub, square, odd.T)
            diagonal = jnp.sum(jnp.where(lane == sub, odd, 0.0), axis=0, keepdims=True)
            diagonals = jnp.where(tile_row == even // 2, diagonal, diagonals)
        else:
            square = jnp.where(lane >= sub, square, 0.0)
        at = even // 2 * size
        packed[at : at + size, :] = square.astype(BF16)
    packed[pairs * size :, :] = diagonals.astype(BF16)


def finish_kernel(
    rep, basis, trans, trans_top, joint, parts, orth, fresh, pool, top, four, own,
    rows, factors, upper, inverse, orth_held, fresh_held, sems,
):
    leaves, slots = basis.shape[0], trans.shape[0]
    came = start_all([(trans, factors), (basis, rows)], sems)
    late = start_all([(parts.at[rep[0]], own)], sems, 3 + leaves)
    square = joint.shape[1:]
    sub = lax.broadcasted_iota(jnp.int32, square, 0)
    lane = lax.broadcasted_iota(jnp.int32, square, 1)
    for node in range(joint.shape[0]):
        both = joint[node]
        upper[node] = jnp.where(lane >= sub, both, 0.0)
        inverse[node] = jnp.where(lane < sub, both, jnp.where(lane == sub, 1.0 / both, 0.0))
    pool[...] = upper[:slots].astype(BF16)
    came[0].wait()
    gone = []
    base, count = 0, leaves
    while count > 1:
        for child in range(count):
            node = base + child
            fresh_held[node] = dot_nt(
                dot_nn(upper[node], factors[node]), inverse[base + count + child // 2]
            )
        base, count = base + count, count // 2
    three = base + 1
    own_three = inverse[three + rep[0] // 2]
    fresh_held[base] = dot_nt(dot_nn(upper[base], factors[base]), own_three)
    gone += start_all([(fresh_held, fresh)], sems, 2)
    came[1].wait()
    for i in range(leaves):
        orth_held[i] = lax.dot_general(
            rows[i], inverse[i].astype(BF16), (((1,), (1,)), ((), ())),
            preferred_element_type=F32,
        ).astype(BF16)
        gone += start_all([(orth_held.at[i], orth.at[i])], sems, 3 + i)
    share = four.shape[1]
    part = pl.ds(pl.multiple_of(rep[0] * share, share), share)
    for c in range(2):
        top[c] = dot_nt(dot_nn(upper[three + c, part, :], trans_top[c]), inverse[three + 2])
    four[0] = upper[three + 2, part, :]
    wait_all(gone + late)


def fold_kernel(add, lead, tail, lead_sum, tail_sum, kept):
    for which, (came, out) in enumerate(((lead, lead_sum), (tail, tail_sum))):
        out[...] = (came[1].astype(F32) + add[which].astype(F32)).astype(BF16)
        kept[which] = came[0]


def half_kernel(row_slot, own, kept, lead_rest, tail_rest, pool, half):
    tiles = lead_rest.shape[0]
    for which, rest in enumerate((lead_rest, tail_rest)):
        for i in range(tiles):
            total = (
                own[which, i].astype(F32) + kept[which, i].astype(F32) + rest[i].astype(F32)
            )
            k = which * tiles + i
            half[k] = jnp.dot(
                pool[row_slot[k]], total.astype(BF16), preferred_element_type=F32
            ).astype(BF16)


def project_kernel(slots, mine, col_node, half, *refs):
    count = 2 * REACH + 1
    pieces, (out, pool, held, sems) = refs[:count], refs[count:]
    rows = pieces[0].shape[0]
    size = out.shape[1]
    for i, piece in enumerate(pieces):
        pool[i * rows : (i + 1) * rows, :] = piece[...]
    sub = lax.broadcasted_iota(jnp.int32, (size, size), 0)
    lane = lax.broadcasted_iota(jnp.int32, (size, size), 1)
    tile_row = lax.broadcasted_iota(jnp.int32, (TILE, size), 0)
    above = (lane >= sub).astype(F32).astype(BF16)
    below = (lane < sub).astype(F32).astype(BF16)
    eye = (lane == sub).astype(F32).astype(BF16)
    pairs = (slots + 1) // 2
    gone = []
    for k in range(out.shape[0]):
        piece, slot = col_node[k] // slots - mine[0] + REACH, col_node[k] % slots
        base = piece * rows
        square = pool[pl.ds(pl.multiple_of(base + slot // 2 * size, TILE), size), :]
        tile = pool[pl.ds(pl.multiple_of(base + pairs * size, TILE), TILE), :].astype(F32)
        diagonal = jnp.sum(jnp.where(tile_row == slot // 2, tile, 0.0), axis=0, keepdims=True)
        spread = jnp.broadcast_to(diagonal, (size, size)).astype(BF16)
        even = lax.dot_general(
            half[k], square * above, (((1,), (1,)), ((), ())), preferred_element_type=F32
        )
        odd = jnp.dot(half[k], square * below + spread * eye, preferred_element_type=F32)
        held[k] = jnp.where(slot % 2 == 0, even, odd).astype(BF16)
        if k % 2 == 1:
            gone += start_all([(held.at[k - 1 : k + 1], out.at[k - 1 : k + 1])], sems, k // 2)
    wait_all(gone)


def shifted(value, steps):
    count = lax.axis_size(ALL)
    return lax.ppermute(value, ALL, [(i, (i + steps) % count) for i in range(count)])


def swapped(value, flip):
    return lax.ppermute(value, "rep", [(i, i ^ flip) for i in range(lax.axis_size("rep"))])


def per_device(leaf_basis, transfer, transfer_top, coupling_parts, row_slot, col_node):
    rank = transfer.shape[1]
    slots = transfer.shape[0]
    leaves = leaf_basis.shape[0]
    reps = lax.axis_size("rep")
    tiles = row_slot.shape[0]
    square = (rank, rank)
    rep = lax.axis_index("rep").astype(jnp.int32).reshape(1)

    parts = coupling_parts.reshape(reps, 2, tiles // 2, rank, rank)
    pair = jax.ShapeDtypeStruct((2, tiles // 2, *square), BF16)
    single = jax.ShapeDtypeStruct((tiles // 2, *square), BF16)
    leaf_basis, transfer, parts = (
        pltpu.with_memory_space_constraint(value, pltpu.HBM)
        for value in (leaf_basis, transfer, parts)
    )
    grams, sent, lead_out, tail_out, add = pl.pallas_call(
        gram_kernel,
        out_shape=[
            jax.ShapeDtypeStruct((slots, *square), F32),
            jax.ShapeDtypeStruct((5 * rank // 8, rank), F32),
            pair,
            pair,
            pair,
        ],
        in_specs=[SMEM] + [ANY] * 3,
        out_specs=[VMEM] * 5,
        scratch_shapes=[
            pltpu.VMEM(leaf_basis.shape, BF16),
            pltpu.VMEM(transfer.shape, F32),
            pltpu.SemaphoreType.DMA((leaves + 7,)),
        ],
        compiler_params=PARAMS,
        name="grams",
    )(rep, leaf_basis, transfer, parts)
    far_b = swapped(sent, 3)
    near, far_a = swapped(sent, 1), swapped(sent, 2)
    lead = swapped(lead_out, 1)
    tail = swapped(tail_out, 2)
    pairs = (slots + 1) // 2
    nodes = (slots + 3, *square)
    joint = pl.pallas_call(
        factor_kernel,
        out_shape=jax.ShapeDtypeStruct(nodes, F32),
        in_specs=[SMEM] + [VMEM] * 6,
        out_specs=VMEM,
        scratch_shapes=[pltpu.VMEM(nodes, F32)],
        compiler_params=PARAMS,
        name="factor",
    )(rep, grams, sent, near, far_a, far_b, transfer_top)
    lead_sum, tail_sum, kept = pl.pallas_call(
        fold_kernel,
        out_shape=[single, single, pair],
        in_specs=[VMEM] * 3,
        out_specs=[VMEM] * 3,
        compiler_params=PARAMS,
        name="fold",
    )(add, lead, tail)
    lead_rest = swapped(lead_sum, 2)
    tail_rest = swapped(tail_sum, 1)
    packed = pl.pallas_call(
        functools.partial(pack_kernel, slots),
        out_shape=jax.ShapeDtypeStruct((pairs * rank + TILE, rank), BF16),
        in_specs=[VMEM],
        out_specs=VMEM,
        compiler_params=PARAMS,
        name="pack",
    )(joint)
    pieces = []
    for offset in range(-REACH, REACH + 1):
        pieces.append(packed if offset == 0 else shifted(packed, -offset))
    share = rank // reps
    orth, fresh, pool, top, four, own = pl.pallas_call(
        finish_kernel,
        out_shape=[
            jax.ShapeDtypeStruct(leaf_basis.shape, BF16),
            jax.ShapeDtypeStruct(transfer.shape, F32),
            jax.ShapeDtypeStruct((slots, *square), BF16),
            jax.ShapeDtypeStruct((2, share, rank), F32),
            jax.ShapeDtypeStruct((1, share, rank), F32),
            pair,
        ],
        in_specs=[SMEM, ANY, ANY, VMEM, VMEM, ANY],
        out_specs=[ANY, ANY, VMEM, VMEM, VMEM, VMEM],
        scratch_shapes=[
            pltpu.VMEM(leaf_basis.shape, BF16),
            pltpu.VMEM(transfer.shape, F32),
            pltpu.VMEM(nodes, F32),
            pltpu.VMEM(nodes, F32),
            pltpu.VMEM(leaf_basis.shape, BF16),
            pltpu.VMEM(transfer.shape, F32),
            pltpu.SemaphoreType.DMA((4 + leaves,)),
        ],
        compiler_params=PARAMS,
        name="finish",
    )(rep, leaf_basis, transfer, transfer_top, joint, parts)
    half = pl.pallas_call(
        half_kernel,
        out_shape=jax.ShapeDtypeStruct((tiles, *square), BF16),
        in_specs=[SMEM] + [VMEM] * 5,
        out_specs=VMEM,
        compiler_params=PARAMS,
        name="half",
    )(row_slot, own, kept, lead_rest, tail_rest, pool)
    mine = lax.axis_index(ALL).astype(jnp.int32).reshape(1)
    projected = pl.pallas_call(
        functools.partial(project_kernel, slots),
        out_shape=jax.ShapeDtypeStruct((tiles, *square), BF16),
        in_specs=[SMEM, SMEM, VMEM] + [VMEM] * (2 * REACH + 1),
        out_specs=ANY,
        scratch_shapes=[
            pltpu.VMEM(((2 * REACH + 1) * packed.shape[0], rank), BF16),
            pltpu.VMEM((tiles, *square), BF16),
            pltpu.SemaphoreType.DMA((tiles // 2,)),
        ],
        compiler_params=PARAMS,
        name="project",
    )(mine, col_node, half, *pieces)
    return (orth, fresh, top, four, projected)


def solution(mesh):
    return jax.shard_map(
        per_device,
        mesh=mesh,
        in_specs=(
            P(ALL, None, None),
            P(ALL, None, None),
            P(("leaf", "dom"), None, None),
            P("rep", ("leaf", "dom"), None, None),
            P(ALL),
            P(ALL),
        ),
        out_specs=(
            P(ALL, None, None),
            P(ALL, None, None),
            P(("leaf", "dom"), "rep", None),
            P(("leaf", "dom"), "rep", None),
            P(ALL, None, None),
        ),
        check_vma=False,
    )
```
